128 devices in a mesh: row: 8 (over x, z_hi), col: 16 (over z_lo, y, core).
Axes of the slice: x: 4, y: 4, z: 4 (z_hi: 2, z_lo: 2; z = z_hi * 2 + z_lo), core: 2. Of those that a mesh axis runs over, the one named last changes fastest.
Arguments:
- blocks: float32 [2048, 16, 1024], P(('row', 'col')), may hold values from -2 to 2
- columns: int32 [1024, 16], replicated, may hold values from 0 to 1023, as said below
- owner_slot: int32 [1024], replicated, may hold values from 0 to 2047, as said below
- keep_mask: int32 [1024, 16], P('row', 'col'), may hold values 0 or 1
Outputs:
- filtered: float32 [1024, 16, 1024], P('row', 'col')
- trace_mean: float32 [], replicated
The draws below stay inside these ranges and needn't reach their ends.
Inputs may be any that keep to these rules, and one draw needn't show every extreme that they name: `columns`: slot g of block row i holds column g * 64 + (i % 64 + o) % 64 for some 0 <= o < 64; in the group g = i // 64 it is i itself. Every block row has its own slot; owner_slot[i] = d * 16 + (i // 64) + r with owner d and r < 1; for every column group some owner fills all 1 of its slots.
All inputs are finite; a program needn't handle non-finite values. No bound on the sum of `keep_mask` on one device may be relied on, other than what follows from the above.
Results may differ from the reference program's by a relative error of at most 0.0003.
Values sent between devices are 32-bit elements; how exact they have to be, the bound alone decides.
A program may use at most 64 MiB of HBM per device.

```python
import jax
import jax.numpy as jnp
from jax import lax

BS = 32
KG = 1
GROUPS = 16
K = 16
NB = 1024
RQ = 64
WIN = 64
SLOT = 1
OWN = 16
OWNERS = 128


def draw_columns(key, part):
    row_numbers = jnp.arange(NB, dtype=jnp.int32)
    scores = jax.random.randint(key, (NB, GROUPS, WIN), 0, 1 << 20) * WIN + jnp.arange(WIN, dtype=jnp.int32)
    own_group = (row_numbers // RQ)[:, None] == jnp.arange(GROUPS, dtype=jnp.int32)[None, :]
    first_offset = (jnp.arange(WIN, dtype=jnp.int32) == 0)[None, None, :]
    scores = jnp.where(own_group[:, :, None] & first_offset, -1, scores)
    offsets = jnp.argsort(scores, axis=2)[:, :, :KG].astype(jnp.int32)
    local_rows = (row_numbers % RQ)[:, None, None]
    result = jnp.arange(GROUPS, dtype=jnp.int32)[None, :, None] * RQ + (local_rows + offsets) % RQ
    return result.reshape(NB, K).astype(jnp.int32)


def draw_owner_slot(key, part):

    def one_bucket(bucket):
        seeded = jax.random.fold_in(key, bucket)
        chosen = jax.random.permutation(jax.random.fold_in(seeded, 1), OWNERS).astype(jnp.int32)
        shuffled = jax.random.permutation(jax.random.fold_in(seeded, 2), RQ).astype(jnp.int32)
        places = jnp.arange(RQ, dtype=jnp.int32)
        values = chosen[places // SLOT] * OWN + bucket * SLOT + places % SLOT
        return (bucket * RQ + shuffled, values)
    targets, values = jax.vmap(one_bucket)(jnp.arange(GROUPS, dtype=jnp.int32))
    return jnp.zeros((NB,), jnp.int32).at[targets.reshape(-1)].set(values.reshape(-1).astype(jnp.int32))


def place_ends(drawn, own_key, least, top_value):
    extent = drawn.shape
    spot = [jax.random.randint(jax.random.fold_in(own_key, axis), (), 0, extent[axis]) for axis in range(len(extent))]
    drawn = drawn.at[tuple(spot)].set(least)
    longest = extent.index(max(extent))
    spot[longest] = (spot[longest] + 1) % extent[longest]
    return drawn.at[tuple(spot)].set(top_value)


def block_scale(own_key, extent, shards, low, top_value):
    gain = 1.0
    for axis_at, parts in shards:
        draws = jax.random.uniform(jax.random.fold_in(jax.random.fold_in(own_key, 6), axis_at), (parts,), jnp.float32, low / len(shards), top_value / len(shards))
        gain = gain * jnp.repeat(jnp.exp(draws), extent[axis_at] // parts).reshape((-1,) + (1,) * (len(extent) - 1 - axis_at))
    return gain


def bell_draw(stream_key, dims, scale, limit, pieces=(), held_as=jnp.bfloat16):
    factor_of = block_scale(stream_key, dims, pieces, -0.22, 0.18) if pieces else 1.0
    drawn = jax.random.normal(stream_key, dims, jnp.float32) * scale * factor_of
    return jnp.minimum(jnp.maximum(drawn, -limit), limit).astype(held_as)


def setup_inputs(seed: int = 0) -> dict:
    splits = jax.random.split(jax.random.key(seed), 5)
    blocks = bell_draw(splits[0], (OWNERS * OWN, K, BS * BS), (KG * 9) ** -0.5, 2.0, ((0, 128),), jnp.float32)
    columns = draw_columns(jax.random.fold_in(splits[4], 71), 0)
    owner_slot = draw_owner_slot(jax.random.fold_in(splits[4], 71), 0)
    keep_mask = place_ends((jax.random.randint(splits[3], (NB, K), 0, 4) < 3).astype(jnp.int32), jax.random.fold_in(splits[3], 1), 0, 1)
    return dict(blocks=blocks, columns=columns, owner_slot=owner_slot, keep_mask=keep_mask)


HIGHEST = lax.Precision.HIGHEST


def reference(blocks, columns, owner_slot, keep_mask):
    total_rows, slot_count = columns.shape
    matrices = blocks[owner_slot].reshape(total_rows, slot_count, BS, BS)

    def one_row(row_number):
        own_columns = columns[row_number]
        inner_blocks = matrices[own_columns]
        inner_columns = columns[own_columns]
        matches = (inner_columns[:, None, :] == own_columns[None, :, None]).astype(matrices.dtype)
        picked = jnp.einsum("mnl,mlxy->mnxy", matches, inner_blocks, precision=HIGHEST)
        return jnp.einsum("mxz,mnzy->nxy", matrices[row_number], picked, precision=HIGHEST)

    batches = jnp.arange(total_rows, dtype=jnp.int32).reshape(-1, 16)
    product = lax.map(jax.vmap(one_row), batches).reshape(total_rows, slot_count, BS, BS)
    diagonal = (columns == jnp.arange(total_rows, dtype=jnp.int32)[:, None]).astype(matrices.dtype)
    traces = jnp.trace(product, axis1=2, axis2=3)
    trace_mean = jnp.sum(diagonal * traces) / total_rows
    filtered = (product * keep_mask[:, :, None, None].astype(matrices.dtype)).reshape(total_rows, slot_count, BS * BS)
    return filtered, trace_mean
```

```python
import functools

import jax
import jax.numpy as jnp
from jax import lax
from jax.experimental import pallas as pl
from jax.experimental.pallas import tpu as pltpu
from jax.sharding import PartitionSpec as P

BS = 32
AREA = BS * BS
SUB, LANES = 8, 128
R, C = 8, 16
HALF = 64
CAP_L = 12
CAP_R = 16
MESH = pl.DeviceIdType.MESH
F32, I32, BF16 = jnp.float32, jnp.int32, jnp.bfloat16
HIGHEST = lax.Precision.HIGHEST


def iota(shape, axis):
    return lax.broadcasted_iota(I32, shape, axis)


def lookup(table, index):
    return jnp.take_along_axis(table, index, axis=1, mode="promise_in_bounds")


def block_products(left, right, out, accumulate):
    def rows(step, carry):
        base = pl.multiple_of(step * (4 * BS), 4 * BS)
        totals = [[None] * 4 for _ in range(4)]
        for z in range(BS):
            tiles = [right[pl.ds(z * BS + 8 * q, 8), :] for q in range(4)]
            for x in range(4):
                factor = jnp.broadcast_to(left[pl.ds(base + x * BS + z, 1), :], (8, LANES))
                for q in range(4):
                    term = factor * tiles[q]
                    totals[x][q] = term if totals[x][q] is None else totals[x][q] + term
        for x in range(4):
            for q in range(4):
                spot = pl.ds(base + x * BS + 8 * q, 8)
                value = totals[x][q]
                out[spot, :] = out[spot, :] + value if accumulate else value
        return carry

    lax.fori_loop(0, BS // 4, rows, 0)


def to_lanes(stacked, out, keep=None):
    for s in range(SUB):
        piece = jnp.transpose(stacked[:, s, :])
        if keep is not None:
            piece = piece * keep
        out[s * LANES : (s + 1) * LANES, :] = piece


def kernel(
    blocks, cols, slots, keep,
    out, aux, panel_out,
    xv, land, agr, dcol, ctb, ct3, tt, lists_v, lists,
    panel, sorted_a, sorted_b, ta, tb, tc, ot,
    lpack, rpack, lland, rland, onehot, tr_src, tr_land,
    in_sem, ct_sem, self_sem, list_sem, out_sem,
    sr_send, sc_send, sr_recv, sc_recv,
    t1_send, t1_recv, ar_send, ac_send, ar_recv, ac_recv, fw_send, fw_recv,
    xl_send, xr_send, xl_recv, xr_recv, tr_send, tr_recv,
):
    r = lax.axis_index("row")
    c = lax.axis_index("col")
    me = r * C + c
    p, q = c % 2, c // 2
    partner = c + 1 - 2 * p

    def remote(src, dst, send, recv, row, col):
        return pltpu.make_async_remote_copy(
            src_ref=src, dst_ref=dst, send_sem=send, recv_sem=recv,
            device_id=(row, col), device_id_type=MESH,
        )

    def drain(ref, sem):
        pltpu.make_async_copy(ref, ref, sem).wait()

    loads = [
        pltpu.make_async_copy(blocks.at[:, :, pl.ds(LANES * t, LANES)], xv.at[:, :, t, :], in_sem.at[t])
        for t in range(SUB)
    ]
    for copy in loads:
        copy.start()
    tables = []
    for b in range(R):
        piece = cols.at[:, pl.ds(LANES * b, LANES)]
        tables.append(pltpu.make_async_copy(piece, ctb.at[b], ct_sem.at[4 * b]))
        tables.append(pltpu.make_async_copy(piece, ct3.at[:, b, :], ct_sem.at[4 * b + 1]))
        tables.append(pltpu.make_async_copy(piece, tt.at[:, 2 * b, :], ct_sem.at[4 * b + 2]))
        tables.append(pltpu.make_async_copy(piece, tt.at[:, 2 * b + 1, :], ct_sem.at[4 * b + 3]))
    for copy in tables:
        copy.start()

    barrier = pltpu.get_barrier_semaphore()

    def greet(k, carry):
        d = (me + k) % (R * C)
        pl.semaphore_signal(barrier, inc=1, device_id=(d // C, d % C), device_id_type=MESH)
        return carry

    lax.fori_loop(1, R * C, greet, 0)
    for copy in loads:
        copy.wait()
    pl.semaphore_wait(barrier, R * C - 1)

    def row_scatter(k, carry):
        rr = (r + k) % R
        for h in range(2):
            g = 2 * rr + h
            remote(xv.at[g, g], agr.at[(p * 8 + q) * 16 + r * 2 + h], sr_send, sr_recv, rr, c).start()
        return carry

    lax.fori_loop(1, R, row_scatter, 0)

    def col_scatter(k, carry):
        g = (c + k) % C
        remote(xv.at[g, g], dcol.at[r * C + c], sc_send, sc_recv, r, g).start()
        return carry

    lax.fori_loop(1, C, col_scatter, 0)

    def exchange(k, carry):
        d = (me + k * 37) % (R * C)
        rr, cc = d // C, d % C
        remote(xv.at[pl.ds(2 * rr, 2), cc], land.at[pl.ds(2 * me, 2)], t1_send, t1_recv, rr, cc).start()
        return carry

    lax.fori_loop(1, R * C, exchange, 0)
    own = [
        pltpu.make_async_copy(xv.at[2 * r, 2 * r], agr.at[(p * 8 + q) * 16 + r * 2], self_sem.at[0]),
        pltpu.make_async_copy(xv.at[2 * r + 1, 2 * r + 1], agr.at[(p * 8 + q) * 16 + r * 2 + 1], self_sem.at[1]),
        pltpu.make_async_copy(xv.at[c, c], dcol.at[r * C + c], self_sem.at[2]),
        pltpu.make_async_copy(xv.at[pl.ds(2 * r, 2), c], land.at[pl.ds(2 * me, 2)], self_sem.at[3]),
    ]
    for copy in own:
        copy.start()

    for copy in tables:
        copy.wait()
    lane8, lane16 = iota((8, LANES), 1), iota((C, LANES), 1)
    sub8, sub16 = iota((8, LANES), 0), iota((C, LANES), 0)
    ones = jnp.ones((LANES, LANES), BF16)

    def prefix(value, axis):
        place, total, step = iota(value.shape, axis), value, 1
        while step < value.shape[axis]:
            total = total + jnp.where(place >= step, pltpu.roll(total, step, axis), 0)
            step *= 2
        return total - value

    def count_before(flags):
        return prefix(flags.astype(I32), 1)

    def count(flags):
        return jnp.sum(flags.astype(I32), axis=1, keepdims=True)

    def count_fast(flags):
        return jnp.dot(flags.astype(BF16), ones, preferred_element_type=F32).astype(I32)

    own_group = 2 * r + (lane16 // HALF)
    mine = ctb[r]
    target = jnp.broadcast_to(ctb[r, pl.ds(c, 1), :], (C, LANES))
    found = lookup(tt[c], mine % LANES)
    hit = (found == target) & (sub16 != c) & (sub16 != own_group)
    rank = count_before(hit)
    total = jnp.broadcast_to(count(hit), (C, LANES))
    first = prefix(total, 0) + rank
    in_pair = jnp.where(sub16 % 2 == 1, pltpu.roll(total, 1, 0), 0) + rank
    spot_a = jnp.minimum(sub16 * CAP_L + rank, C * CAP_L - 1)
    spot_b = jnp.minimum((sub16 // 2) * CAP_R + in_pair, R * CAP_R - 1)
    spots = spot_a + 256 * spot_b
    rows = iota((LANES, LANES), 0)
    chosen = jnp.zeros((LANES, LANES), I32)
    picks = jnp.zeros((LANES, LANES), I32)
    order = jnp.where(hit, first, -1)
    for m in range(C):
        spread = rows == order[m : m + 1, :]
        chosen = jnp.where(spread, 1, chosen)
        picks = jnp.where(spread, spots[m : m + 1, :], picks)
    onehot[...] = chosen.astype(BF16)
    picks = jnp.broadcast_to(jnp.sum(picks, axis=1, keepdims=True), (LANES, LANES))
    picks = jnp.transpose(picks)[0:8, :]

    owner = slots[pl.ds(r, 1), :] // C
    far_owner = lookup(
        jnp.broadcast_to(slots[pl.ds(q, 1), :] // C, (8, LANES)),
        jnp.broadcast_to(ctb[r, pl.ds(c, 1), :] % LANES, (8, LANES)),
    )
    owner8 = jnp.broadcast_to(owner, (8, LANES))
    half = lane8 // HALF
    o_col, o_row = owner8 % C, owner8 // C
    at_land = 2 * owner8 + half
    at_agr = (((o_col % 2) * 8 + o_col // 2) * 8 + o_row) * 2 + half
    head = jnp.where(sub8 == 0, at_land, jnp.where(sub8 == 1, at_agr, far_owner))
    head = jnp.where(sub8 == 3, picks % 256, jnp.where(sub8 == 4, picks // 256, head))
    lists_v[0:8, :] = head

    left_index = jnp.broadcast_to(ctb[r, pl.ds(c, 1), :] % LANES, (C, LANES))
    left_found = lookup(ctb[q], left_index)
    left_hit = (left_found == mine) & (sub16 != c) & (own_group != c)
    left_rank = count_before(left_hit)
    left_list = jnp.zeros((C, LANES), I32)
    for k in range(CAP_L):
        value = jnp.sum(jnp.where(left_hit & (left_rank == k), lane16, 0), axis=1, keepdims=True)
        left_list = jnp.where(lane16 == k, value, left_list)
    lists_v[8:24, :] = left_list

    right_target = ct3[c]
    right_table = jnp.broadcast_to(ct3[c, pl.ds(r, 1), :], (8, LANES))
    their_group = 2 * sub8 + half
    right_list = jnp.zeros((8, LANES), I32)
    flags, places, ranks = [], [], []
    for h in range(2):
        m = 2 * r + h
        place = ct3[m] % LANES
        right_hit = (lookup(right_table, place) == right_target) & (m != c) & (their_group != m)
        right_rank = count_before(right_hit)
        if h == 1:
            right_rank = right_rank + count(flags[0])
        flags.append(right_hit)
        places.append(place)
        ranks.append(right_rank)
    for k in range(CAP_R):
        value = sum(
            jnp.sum(jnp.where(flags[h] & (ranks[h] == k), places[h], 0), axis=1, keepdims=True)
            for h in range(2)
        )
        right_list = jnp.where(lane8 == k, value, right_list)
    lists_v[24:32, :] = right_list
    to_smem = pltpu.make_async_copy(lists_v, lists, list_sem)
    to_smem.start()

    even = sub16 % 2 == 0

    def survey(step, worst):
        row, col = step // C, step % C
        theirs = ctb[row]
        wanted = jnp.broadcast_to(ct3[col, pl.ds(row, 1), :], (C, LANES))
        seen = lookup(tt[col], theirs % LANES)
        group = 2 * row + (lane16 // HALF)
        used = count_fast((seen == wanted) & (sub16 != col) & (sub16 != group))
        pair = jnp.where(even, used + pltpu.roll(used, C - 1, 0), 0)
        whole = jnp.sum(used, axis=0, keepdims=True)
        over = jnp.maximum(used - CAP_L, pair - CAP_R)
        return jnp.maximum(worst, jnp.maximum(over, whole - LANES))

    worst = lax.fori_loop(0, R * C, survey, jnp.full((C, LANES), -1, I32))
    to_smem.wait()
    for copy in own:
        copy.wait()

    piece = agr.at[pl.ds((p * 8 + q) * 16, 16)]
    column_piece = dcol.at[pl.ds(r * C, C)]
    drain(agr.at[pl.ds(0, 2 * (R - 1))], sr_recv)
    drain(dcol.at[pl.ds(0, C - 1)], sc_recv)

    def row_gather(k, carry):
        cc = (c + 2 * k) % C
        remote(piece, piece, ar_send, ar_recv, r, cc).start()
        return carry

    lax.fori_loop(1, C // 2, row_gather, 0)

    def col_gather(k, carry):
        remote(column_piece, column_piece, ac_send, ac_recv, (r + k) % R, c).start()
        return carry

    lax.fori_loop(1, R, col_gather, 0)

    drain(land.at[pl.ds(0, 2 * (R * C - 1))], t1_recv)

    def collect(i, carry):
        panel[i] = land[jnp.clip(lists[0, i], 0, 2 * R * C - 1)]
        return carry

    lax.fori_loop(0, LANES, collect, 0, unroll=8)

    def pack_left(d, carry):
        for k in range(CAP_L):
            lpack[d * CAP_L + k] = panel[jnp.clip(lists[8 + d, k], 0, LANES - 1)]
        return carry

    lax.fori_loop(0, C, pack_left, 0)

    def send_left(k, carry):
        cc = (c + k) % C
        remote(lpack.at[pl.ds(cc * CAP_L, CAP_L)], lland.at[pl.ds(c * CAP_L, CAP_L)], xl_send, xl_recv, r, cc).start()
        return carry

    lax.fori_loop(1, C, send_left, 0)

    def pack_right(d, carry):
        for k in range(CAP_R):
            rpack[d * CAP_R + k] = panel[jnp.clip(lists[24 + d, k], 0, LANES - 1)]
        return carry

    lax.fori_loop(0, R, pack_right, 0)

    def send_right(k, carry):
        rr = (r + k) % R
        remote(rpack.at[pl.ds(rr * CAP_R, CAP_R)], rland.at[pl.ds(r * CAP_R, CAP_R)], xr_send, xr_recv, rr, c).start()
        return carry

    lax.fori_loop(1, R, send_right, 0)
    keep_left = pltpu.make_async_copy(
        lpack.at[pl.ds(c * CAP_L, CAP_L)], lland.at[pl.ds(c * CAP_L, CAP_L)], self_sem.at[4]
    )
    keep_right = pltpu.make_async_copy(
        rpack.at[pl.ds(r * CAP_R, CAP_R)], rland.at[pl.ds(r * CAP_R, CAP_R)], self_sem.at[5]
    )
    keep_left.start()
    keep_right.start()
    save = pltpu.make_async_copy(panel, panel_out, out_sem)
    save.start()

    drain(agr.at[pl.ds(0, 16 * (C // 2 - 1))], ar_recv)
    forward = remote(agr.at[pl.ds(p * 128, 128)], agr.at[pl.ds(p * 128, 128)], fw_send, fw_recv, r, partner)
    forward.start()

    to_lanes(panel, tb)
    drain(dcol.at[pl.ds(0, C * (R - 1))], ac_recv)

    def collect_column(i, carry):
        sorted_b[i] = dcol[jnp.clip(lists[2, i], 0, R * C - 1)]
        return carry

    lax.fori_loop(0, LANES, collect_column, 0, unroll=8)
    to_lanes(sorted_b, tc)
    block_products(tb, tc, ot, False)
    forward.wait()

    def collect_row(i, carry):
        sorted_a[i] = agr[jnp.clip(lists[1, i], 0, 2 * R * C - 1)]
        return carry

    lax.fori_loop(0, LANES, collect_row, 0, unroll=8)
    lane1 = iota((1, LANES), 1)
    group1 = 2 * r + lane1 // HALF
    to_lanes(sorted_a, ta, (group1 != c).astype(F32))
    block_products(ta, tb, ot, True)

    keep_left.wait()
    keep_right.wait()
    drain(lland.at[pl.ds(0, (C - 1) * CAP_L)], xl_recv)
    drain(rland.at[pl.ds(0, (R - 1) * CAP_R)], xr_recv)

    def collect_pairs(i, carry):
        sorted_a[i] = lland[jnp.clip(lists[3, i], 0, C * CAP_L - 1)]
        sorted_b[i] = rland[jnp.clip(lists[4, i], 0, R * CAP_R - 1)]
        return carry

    lax.fori_loop(0, LANES, collect_pairs, 0, unroll=8)
    to_lanes(sorted_a, ta)
    to_lanes(sorted_b, tc)
    block_products(ta, tc, tb, False)
    spread = onehot[...]
    for s in range(SUB):
        spot = slice(s * LANES, (s + 1) * LANES)
        value = tb[spot, :]
        high = value.astype(BF16)
        rest = value - high.astype(F32)
        middle = rest.astype(BF16)
        low = (rest - middle.astype(F32)).astype(BF16)
        moved = jnp.dot(low, spread, preferred_element_type=F32)
        moved = moved + jnp.dot(middle, spread, preferred_element_type=F32)
        moved = moved + jnp.dot(high, spread, preferred_element_type=F32)
        ot[spot, :] = ot[spot, :] + moved

    diagonal = ot[0:1, :]
    for x in range(1, BS):
        diagonal = diagonal + ot[33 * x : 33 * x + 1, :]
    partial = jnp.sum(jnp.where(group1 == c, diagonal, 0.0), axis=1, keepdims=True)
    tr_src[...] = jnp.broadcast_to(partial, (SUB, LANES))
    source = q == r

    @pl.when(source)
    def _():
        tr_land[c] = jnp.broadcast_to(partial, (SUB, LANES))

        def tell(k, carry):
            d = (me + k) % (R * C)
            remote(tr_src, tr_land.at[c], tr_send, tr_recv, d // C, d % C).start()
            return carry

        lax.fori_loop(1, R * C, tell, 0)

    kept = keep[...].astype(F32)
    for s in range(SUB):
        spot = slice(s * LANES, (s + 1) * LANES)
        out[:, spot] = jnp.transpose(ot[spot, :] * kept)

    @pl.when(source)
    def _():
        drain(tr_land.at[pl.ds(0, C - 1)], tr_recv)
        drain(land.at[pl.ds(0, R * C - 1)], tr_send)

    @pl.when(jnp.logical_not(source))
    def _():
        drain(tr_land, tr_recv)

    trace = tr_land[0]
    for k in range(1, C):
        trace = trace + tr_land[k]
    limit = jnp.max(worst, axis=0, keepdims=True)
    limit = jnp.max(limit, axis=1, keepdims=True)
    aux[...] = jnp.where(sub8 == 0, trace / (R * LANES), jnp.broadcast_to(limit, (8, LANES)).astype(F32))

    save.wait()
    drain(agr.at[pl.ds(0, 2 * (R - 1))], sr_send)
    drain(dcol.at[pl.ds(0, C - 1)], sc_send)
    drain(land.at[pl.ds(0, 2 * (R * C - 1))], t1_send)
    drain(agr.at[pl.ds(0, 16 * (C // 2 - 1))], ar_send)
    drain(dcol.at[pl.ds(0, C * (R - 1))], ac_send)
    drain(lland.at[pl.ds(0, (C - 1) * CAP_L)], xl_send)
    drain(rland.at[pl.ds(0, (R - 1) * CAP_R)], xr_send)


def sparse_product(blocks, cols, slots, keep):
    tile = (SUB, LANES)
    dma = pltpu.SemaphoreType.DMA
    wide = pltpu.VMEM((AREA, LANES), F32)
    batch = pltpu.VMEM((LANES,) + tile, F32)
    vmem = pl.BlockSpec(memory_space=pltpu.VMEM)
    hbm = pl.BlockSpec(memory_space=pl.ANY)
    return pl.pallas_call(
        kernel,
        out_shape=(
            jax.ShapeDtypeStruct((LANES, AREA), F32),
            jax.ShapeDtypeStruct(tile, F32),
            jax.ShapeDtypeStruct((LANES,) + tile, F32),
        ),
        in_specs=[hbm, hbm, vmem, vmem],
        out_specs=(vmem, vmem, hbm),
        scratch_shapes=[
            pltpu.VMEM((C, C) + tile, F32),
            pltpu.VMEM((2 * R * C,) + tile, F32),
            pltpu.VMEM((2 * R * C,) + tile, F32),
            pltpu.VMEM((R * C,) + tile, F32),
            pltpu.VMEM((R, C, LANES), I32),
            pltpu.VMEM((C, R, LANES), I32),
            pltpu.VMEM((C, C, LANES), I32),
            pltpu.VMEM((32, LANES), I32),
            pltpu.SMEM((32, LANES), I32),
            batch, batch, batch,
            wide, wide, wide, wide,
            pltpu.VMEM((C * CAP_L,) + tile, F32),
            pltpu.VMEM((R * CAP_R,) + tile, F32),
            pltpu.VMEM((C * CAP_L,) + tile, F32),
            pltpu.VMEM((R * CAP_R,) + tile, F32),
            pltpu.VMEM((LANES, LANES), BF16),
            pltpu.VMEM(tile, F32),
            pltpu.VMEM((C,) + tile, F32),
            dma((SUB,)), dma((4 * R,)), dma((6,)), dma, dma,
        ] + [dma] * 18,
        compiler_params=pltpu.CompilerParams(collective_id=0, has_side_effects=True),
    )(blocks, cols, slots, keep)


def dense_product(panel, columns, keep):
    r, c = lax.axis_index("row"), lax.axis_index("col")
    mine = lax.dynamic_slice_in_dim(columns, r * LANES, LANES)
    target = lax.dynamic_slice_in_dim(mine, c, 1, 1)[:, 0]
    far_all = lax.dynamic_slice_in_dim(columns, c, 1, 1)[:, 0]
    flat = panel.reshape(LANES, AREA)

    def around(value, axis):
        size = lax.axis_size(axis)
        return lax.ppermute(value, axis, [((i + 1) % size, i) for i in range(size)])

    def gather(step, carry):
        rights, moving = carry
        rights = lax.dynamic_update_slice_in_dim(rights, moving[None], (r + step) % R, 0)
        return rights, around(moving, "row")

    rights, _ = lax.fori_loop(0, R, gather, (jnp.zeros((R, LANES, AREA), F32), flat))
    rights = rights.reshape(R * LANES, AREA)

    def advance(step, carry):
        totals, left = carry
        m = (c + step) % C
        inner = lax.dynamic_slice_in_dim(mine, m, 1, 1)[:, 0]
        match = (far_all[inner] == target).astype(F32)
        right = rights[inner] * match[:, None]
        term = jnp.einsum(
            "nxz,nzy->nxy", left.reshape(LANES, BS, BS), right.reshape(LANES, BS, BS), precision=HIGHEST
        )
        return totals + term, around(left, "col")

    totals, _ = lax.fori_loop(0, C, advance, (jnp.zeros((LANES, BS, BS), F32), flat))
    ids = r * LANES + jnp.arange(LANES, dtype=I32)
    traces = jnp.trace(totals, axis1=1, axis2=2)
    trace = jnp.full((8, LANES), jnp.sum(jnp.where(target == ids, traces, 0.0)))
    for axis in ("row", "col"):
        def add(step, carry):
            total, moving = carry
            moving = around(moving, axis)
            return total + moving, moving
        trace, _ = lax.fori_loop(1, lax.axis_size(axis), add, (trace, trace))
    filtered = totals.reshape(LANES, AREA) * keep.reshape(LANES, 1).astype(F32)
    return filtered, trace[0, 0] / (R * LANES)


def shards(blocks, columns, owner_slot, keep_mask):
    keep = keep_mask.T
    filtered, aux, panel = sparse_product(blocks, columns.T, owner_slot.reshape(R, LANES), keep)
    filtered, trace = lax.cond(
        aux[1, 0] > 0,
        lambda f, t, s: dense_product(s, columns, keep),
        lambda f, t, s: (f, t),
        filtered, aux[0, 0], panel,
    )
    return filtered.reshape(LANES, 1, AREA), trace


def solution(mesh):
    in_specs = (P(("row", "col"), None, None), P(), P(), P("row", "col"))
    out_specs = (P("row", "col", None), P())
    return jax.shard_map(shards, mesh=mesh, in_specs=in_specs, out_specs=out_specs, check_vma=False)
```

```python
import functools

import jax
import jax.numpy as jnp
from jax import lax
from jax.experimental import pallas as pl
from jax.experimental.pallas import tpu as pltpu
from jax.sharding import PartitionSpec as P

BS = 32
AREA = BS * BS
SUB, LANES = 8, 128
R, C = 8, 16
HALF = 64
CAP_L = 12
CAP_R = 16
MESH = pl.DeviceIdType.MESH
F32, I32, BF16 = jnp.float32, jnp.int32, jnp.bfloat16
HIGHEST = lax.Precision.HIGHEST


def iota(shape, axis):
    return lax.broadcasted_iota(I32, shape, axis)


def lookup(table, index):
    return jnp.take_along_axis(table, index, axis=1, mode="promise_in_bounds")


def block_products(left, right, out, accumulate):
    def rows(step, carry):
        base = pl.multiple_of(step * (4 * BS), 4 * BS)
        totals = [[None] * 4 for _ in range(4)]
        for z in range(BS):
            tiles = [right[pl.ds(z * BS + 8 * q, 8), :] for q in range(4)]
            for x in range(4):
                factor = jnp.broadcast_to(left[pl.ds(base + x * BS + z, 1), :], (8, LANES))
                for q in range(4):
                    term = factor * tiles[q]
                    totals[x][q] = term if totals[x][q] is None else totals[x][q] + term
        for x in range(4):
            for q in range(4):
                spot = pl.ds(base + x * BS + 8 * q, 8)
                value = totals[x][q]
                out[spot, :] = out[spot, :] + value if accumulate else value
        return carry

    lax.fori_loop(0, BS // 4, rows, 0)


def to_lanes(stacked, out, keep=None):
    for s in range(SUB):
        piece = jnp.transpose(stacked[:, s, :])
        if keep is not None:
            piece = piece * keep
        out[s * LANES : (s + 1) * LANES, :] = piece


def kernel(
    blocks, cols, slots, keep,
    out, mean_out, over_out, panel_out,
    xv, land, agr, dcol, ctb, ct3, tt, lists_v, lists,
    panel, sorted_a, sorted_b, ta, tb, tc, ot, tr_all,
    lpack, rpack, lland, rland, onehot, tr_src, tr_land,
    in_sem, ct_sem, self_sem, list_sem, out_sem,
    sr_send, sc_send, sr_recv, sc_recv,
    t1_send, t1_recv, ar_send, ac_send, ar_recv, ac_recv, fw_send, fw_recv,
    xl_send, xr_send, xl_recv, xr_recv, tr_send, tr_recv,
):
    r = lax.axis_index("row")
    c = lax.axis_index("col")
    me = r * C + c
    p, q = c % 2, c // 2
    partner = c + 1 - 2 * p

    def remote(src, dst, send, recv, row, col):
        return pltpu.make_async_remote_copy(
            src_ref=src, dst_ref=dst, send_sem=send, recv_sem=recv,
            device_id=(row, col), device_id_type=MESH,
        )

    def drain(ref, sem):
        pltpu.make_async_copy(ref, ref, sem).wait()

    barrier = pltpu.get_barrier_semaphore()

    def greet(k, carry):
        d = (me + k) % (R * C)
        pl.semaphore_signal(barrier, inc=1, device_id=(d // C, d % C), device_id_type=MESH)
        return carry

    lax.fori_loop(1, R * C, greet, 0)

    loads = [
        pltpu.make_async_copy(blocks.at[:, :, pl.ds(LANES * t, LANES)], xv.at[:, :, t, :], in_sem.at[t])
        for t in range(SUB)
    ]
    for copy in loads:
        copy.start()
    tables = []
    for b in range(R):
        piece = cols.at[:, pl.ds(LANES * b, LANES)]
        tables.append(pltpu.make_async_copy(piece, ctb.at[b], ct_sem.at[4 * b]))
        tables.append(pltpu.make_async_copy(piece, ct3.at[:, b, :], ct_sem.at[4 * b + 1]))
        tables.append(pltpu.make_async_copy(piece, tt.at[:, 2 * b, :], ct_sem.at[4 * b + 2]))
        tables.append(pltpu.make_async_copy(piece, tt.at[:, 2 * b + 1, :], ct_sem.at[4 * b + 3]))
    for copy in tables:
        copy.start()

    for copy in tables:
        copy.wait()
    lane8, lane16 = iota((8, LANES), 1), iota((C, LANES), 1)
    sub8, sub16 = iota((8, LANES), 0), iota((C, LANES), 0)
    def prefix(value, axis):
        place, total, step = iota(value.shape, axis), value, 1
        while step < value.shape[axis]:
            total = total + jnp.where(place >= step, pltpu.roll(total, step, axis), 0)
            step *= 2
        return total - value

    def count_before(flags):
        return prefix(flags.astype(I32), 1)

    def count(flags):
        return jnp.sum(flags.astype(I32), axis=1, keepdims=True)

    own_group = 2 * r + (lane16 // HALF)
    mine = ctb[r]
    target = jnp.broadcast_to(ctb[r, pl.ds(c, 1), :], (C, LANES))
    found = lookup(tt[c], mine % LANES)
    hit = (found == target) & (sub16 != c) & (sub16 != own_group)
    rank = count_before(hit)
    total = jnp.broadcast_to(count(hit), (C, LANES))
    first = prefix(total, 0) + rank
    in_pair = jnp.where(sub16 % 2 == 1, pltpu.roll(total, 1, 0), 0) + rank
    spot_a = jnp.minimum(sub16 * CAP_L + rank, C * CAP_L - 1)
    spot_b = jnp.minimum((sub16 // 2) * CAP_R + in_pair, R * CAP_R - 1)
    spots = spot_a + 256 * spot_b
    rows = iota((LANES, LANES), 0)
    chosen = jnp.zeros((LANES, LANES), I32)
    picks = jnp.zeros((LANES, LANES), I32)
    order = jnp.where(hit, first, -1)
    for m in range(C):
        spread = rows == order[m : m + 1, :]
        chosen = jnp.where(spread, 1, chosen)
        picks = jnp.where(spread, spots[m : m + 1, :], picks)
    onehot[...] = chosen.astype(BF16)
    picks = jnp.broadcast_to(jnp.sum(picks, axis=1, keepdims=True), (LANES, LANES))
    picks = jnp.transpose(picks)[0:8, :]

    owner = slots[pl.ds(r, 1), :] // C
    far_owner = lookup(
        jnp.broadcast_to(slots[pl.ds(q, 1), :] // C, (8, LANES)),
        jnp.broadcast_to(ctb[r, pl.ds(c, 1), :] % LANES, (8, LANES)),
    )
    owner8 = jnp.broadcast_to(owner, (8, LANES))
    half = lane8 // HALF
    o_col, o_row = owner8 % C, owner8 // C
    at_land = 2 * owner8 + half
    at_agr = (((o_col % 2) * 4 + (o_col // 2) % 4) * 2 + o_col // 8) * 16 + o_row * 2 + half
    head = jnp.where(sub8 == 0, at_land, jnp.where(sub8 == 1, at_agr, far_owner))
    head = jnp.where(sub8 == 3, picks % 256, jnp.where(sub8 == 4, picks // 256, head))
    lists_v[0:8, :] = head

    left_index = jnp.broadcast_to(ctb[r, pl.ds(c, 1), :] % LANES, (C, LANES))
    left_found = lookup(ctb[q], left_index)
    left_hit = (left_found == mine) & (sub16 != c) & (own_group != c)
    left_rank = count_before(left_hit)
    left_list = jnp.zeros((C, LANES), I32)
    for k in range(CAP_L):
        value = jnp.sum(jnp.where(left_hit & (left_rank == k), lane16, 0), axis=1, keepdims=True)
        left_list = jnp.where(lane16 == k, value, left_list)
    lists_v[8:24, :] = left_list

    right_target = ct3[c]
    right_table = jnp.broadcast_to(ct3[c, pl.ds(r, 1), :], (8, LANES))
    their_group = 2 * sub8 + half
    right_list = jnp.zeros((8, LANES), I32)
    flags, places, ranks = [], [], []
    for h in range(2):
        m = 2 * r + h
        place = ct3[m] % LANES
        right_hit = (lookup(right_table, place) == right_target) & (m != c) & (their_group != m)
        right_rank = count_before(right_hit)
        if h == 1:
            right_rank = right_rank + count(flags[0])
        flags.append(right_hit)
        places.append(place)
        ranks.append(right_rank)
    for k in range(CAP_R):
        value = sum(
            jnp.sum(jnp.where(flags[h] & (ranks[h] == k), places[h], 0), axis=1, keepdims=True)
            for h in range(2)
        )
        right_list = jnp.where(lane8 == k, value, right_list)
    lists_v[24:32, :] = right_list
    to_smem = pltpu.make_async_copy(lists_v, lists, list_sem)
    to_smem.start()

    for copy in loads:
        copy.wait()
    pl.semaphore_wait(barrier, R * C - 1)

    row_spot = ((p * 4 + q % 4) * 2 + c // 8) * 16 + r * 2
    col_spot = r * C + c

    def row_scatter(k, carry):
        rr, cc = (r + k % R) % R, (c + 8 * (k // R)) % C
        for h in range(2):
            g = 2 * rr + h
            remote(xv.at[g, g], agr.at[row_spot + h], sr_send, sr_recv, rr, cc).start()
        return carry

    lax.fori_loop(1, 2 * R, row_scatter, 0)

    def col_scatter(k, carry):
        g, rr = (c + k % C) % C, r + (k // C) * (1 - 2 * (r % 2))
        remote(xv.at[g, g], dcol.at[col_spot], sc_send, sc_recv, rr, g).start()
        return carry

    lax.fori_loop(1, 2 * C, col_scatter, 0)

    def exchange(k, carry):
        d = (me + k * 37) % (R * C)
        rr, cc = d // C, d % C
        remote(xv.at[pl.ds(2 * rr, 2), cc], land.at[pl.ds(2 * me, 2)], t1_send, t1_recv, rr, cc).start()
        return carry

    lax.fori_loop(1, R * C, exchange, 0)
    own = [
        pltpu.make_async_copy(xv.at[2 * r, 2 * r], agr.at[row_spot], self_sem.at[0]),
        pltpu.make_async_copy(xv.at[2 * r + 1, 2 * r + 1], agr.at[row_spot + 1], self_sem.at[1]),
        pltpu.make_async_copy(xv.at[c, c], dcol.at[r * C + c], self_sem.at[2]),
        pltpu.make_async_copy(xv.at[pl.ds(2 * r, 2), c], land.at[pl.ds(2 * me, 2)], self_sem.at[3]),
    ]
    for copy in own:
        copy.start()

    for copy in own:
        copy.wait()
    piece = agr.at[pl.ds((p * 4 + q % 4) * 32, 32)]
    column_piece = dcol.at[pl.ds((r // 2) * 32, 32)]
    drain(agr.at[pl.ds(0, 30)], sr_recv)
    drain(dcol.at[pl.ds(0, 31)], sc_recv)

    def row_gather(k, carry):
        cc = (c // 8) * 8 + (c % 8 + 2 * k) % 8
        remote(piece, piece, ar_send, ar_recv, r, cc).start()
        return carry

    lax.fori_loop(1, 4, row_gather, 0)

    def col_gather(k, carry):
        remote(column_piece, column_piece, ac_send, ac_recv, (r + 2 * k) % R, c).start()
        return carry

    lax.fori_loop(1, 4, col_gather, 0)

    even = sub16 % 2 == 0
    worst = jnp.full((C, LANES), -1, I32)
    for col in range(C):
        wanted = jnp.broadcast_to(ctb[r, col : col + 1, :], (C, LANES))
        seen = lookup(tt[col], mine % LANES)
        used = jnp.broadcast_to(count((seen == wanted) & (sub16 != col) & (sub16 != own_group)), (C, LANES))
        pair = jnp.where(even, used + pltpu.roll(used, C - 1, 0), 0)
        whole = jnp.sum(used, axis=0, keepdims=True)
        worst = jnp.maximum(worst, jnp.maximum(jnp.maximum(used - CAP_L, pair - CAP_R), whole - LANES))
    to_smem.wait()
    drain(land.at[pl.ds(0, 2 * (R * C - 1))], t1_recv)

    def collect(i, carry):
        panel[i] = land[jnp.clip(lists[0, i], 0, 2 * R * C - 1)]
        return carry

    lax.fori_loop(0, LANES, collect, 0, unroll=8)

    def pack_left(d, carry):
        for k in range(CAP_L):
            lpack[d * CAP_L + k] = panel[jnp.clip(lists[8 + d, k], 0, LANES - 1)]
        return carry

    lax.fori_loop(0, C, pack_left, 0)

    def send_left(cc):
        src, dst = lpack.at[pl.ds(cc * CAP_L, CAP_L)], lland.at[pl.ds(c * CAP_L, CAP_L)]
        remote(src, dst, xl_send, xl_recv, r, cc).start()

    for h in range(2):
        pl.when(c != 2 * r + h)(functools.partial(send_left, 2 * r + h))

    def send_left_rest(k, carry):
        cc = (c + k) % C
        pl.when(cc // 2 != r)(functools.partial(send_left, cc))
        return carry

    lax.fori_loop(1, C, send_left_rest, 0)

    def pack_right(d, carry):
        for k in range(CAP_R):
            rpack[d * CAP_R + k] = panel[jnp.clip(lists[24 + d, k], 0, LANES - 1)]
        return carry

    lax.fori_loop(0, R, pack_right, 0)

    def send_right(rr):
        src, dst = rpack.at[pl.ds(rr * CAP_R, CAP_R)], rland.at[pl.ds(r * CAP_R, CAP_R)]
        remote(src, dst, xr_send, xr_recv, rr, c).start()

    source = q == r
    pl.when(jnp.logical_not(source))(functools.partial(send_right, q))

    def send_right_rest(k, carry):
        rr = (r + k) % R
        pl.when(rr != q)(functools.partial(send_right, rr))
        return carry

    lax.fori_loop(1, R, send_right_rest, 0)
    keep_left = pltpu.make_async_copy(
        lpack.at[pl.ds(c * CAP_L, CAP_L)], lland.at[pl.ds(c * CAP_L, CAP_L)], self_sem.at[4]
    )
    keep_right = pltpu.make_async_copy(
        rpack.at[pl.ds(r * CAP_R, CAP_R)], rland.at[pl.ds(r * CAP_R, CAP_R)], self_sem.at[5]
    )
    keep_left.start()
    keep_right.start()
    save = pltpu.make_async_copy(panel, panel_out, out_sem)
    save.start()

    drain(agr.at[pl.ds(0, 96)], ar_recv)
    forward = remote(agr.at[pl.ds(p * 128, 128)], agr.at[pl.ds(p * 128, 128)], fw_send, fw_recv, r, partner)
    forward.start()

    to_lanes(panel, tb)
    drain(dcol.at[pl.ds(0, 96)], ac_recv)

    def collect_column(i, carry):
        sorted_b[i] = dcol[jnp.clip(lists[2, i], 0, R * C - 1)]
        return carry

    lax.fori_loop(0, LANES, collect_column, 0, unroll=8)
    to_lanes(sorted_b, tc)
    block_products(tb, tc, ot, False)
    forward.wait()

    def collect_row(i, carry):
        sorted_a[i] = agr[jnp.clip(lists[1, i], 0, 2 * R * C - 1)]
        return carry

    lax.fori_loop(0, LANES, collect_row, 0, unroll=8)
    lane1 = iota((1, LANES), 1)
    group1 = 2 * r + lane1 // HALF
    to_lanes(sorted_a, ta, (group1 != c).astype(F32))
    block_products(ta, tb, ot, True)

    keep_left.wait()
    keep_right.wait()
    drain(lland.at[pl.ds(0, (C - 1) * CAP_L)], xl_recv)
    drain(rland.at[pl.ds(0, (R - 1) * CAP_R)], xr_recv)

    def collect_pairs(i, carry):
        sorted_a[i] = lland[jnp.clip(lists[3, i], 0, C * CAP_L - 1)]
        sorted_b[i] = rland[jnp.clip(lists[4, i], 0, R * CAP_R - 1)]
        return carry

    lax.fori_loop(0, LANES, collect_pairs, 0, unroll=8)
    to_lanes(sorted_a, ta)
    to_lanes(sorted_b, tc)

    @pl.when(source)
    def _():
        diagonal = ot[0:1, :]
        for x in range(1, BS):
            diagonal = diagonal + ot[33 * x : 33 * x + 1, :]
        totals = jnp.zeros((BS, LANES), F32)
        for x in range(BS):
            totals = totals + ta[BS * x : BS * (x + 1), :] * tc[pl.ds(x, BS, stride=BS), :]
        pairs = jnp.sum(totals, axis=0, keepdims=True)
        inside = jnp.broadcast_to((group1 == c).astype(BF16), (8, LANES))
        weight = lax.dot_general(inside, onehot[...], (((1,), (1,)), ((), ())), preferred_element_type=F32)
        partial = jnp.sum(
            jnp.where(group1 == c, diagonal, 0.0) + pairs * weight[0:1, :], axis=1, keepdims=True
        )
        most = jnp.max(jnp.max(worst, axis=0, keepdims=True), axis=1, keepdims=True).astype(F32)
        told = jnp.where(lane1 < HALF, jnp.broadcast_to(partial, (1, LANES)), jnp.broadcast_to(most, (1, LANES)))
        tr_src[...] = told
        tr_land[c] = told

        def tell(k, carry):
            d = (me + k) % (R * C)
            remote(tr_src, tr_land.at[c], tr_send, tr_recv, d // C, d % C).start()
            return carry

        lax.fori_loop(1, R * C, tell, 0)

    block_products(ta, tc, tb, False)
    spread = onehot[...]
    for s in range(SUB):
        spot = slice(s * LANES, (s + 1) * LANES)
        value = tb[spot, :]
        high = value.astype(BF16)
        rest = value - high.astype(F32)
        middle = rest.astype(BF16)
        low = (rest - middle.astype(F32)).astype(BF16)
        moved = jnp.dot(low, spread, preferred_element_type=F32)
        moved = moved + jnp.dot(middle, spread, preferred_element_type=F32)
        moved = moved + jnp.dot(high, spread, preferred_element_type=F32)
        ot[spot, :] = ot[spot, :] + moved

    kept = keep[...].astype(F32)
    for s in range(SUB):
        spot = slice(s * LANES, (s + 1) * LANES)
        out[:, s, :] = jnp.transpose(ot[spot, :] * kept)

    @pl.when(source)
    def _():
        drain(tr_land.at[pl.ds(0, C - 1)], tr_recv)
        drain(tr_all, tr_send)

    @pl.when(jnp.logical_not(source))
    def _():
        drain(tr_land, tr_recv)

    trace, most = tr_land[0], tr_land[0]
    for k in range(1, C):
        trace = trace + tr_land[k]
        most = jnp.maximum(most, tr_land[k])
    mean_out[...] = trace[:, 0:1] / (R * LANES)
    over_out[...] = most[:, HALF : HALF + 1]

    save.wait()
    drain(agr.at[pl.ds(0, 30)], sr_send)
    drain(dcol.at[pl.ds(0, 31)], sc_send)
    drain(land.at[pl.ds(0, 2 * (R * C - 1))], t1_send)
    drain(agr.at[pl.ds(0, 96)], ar_send)
    drain(dcol.at[pl.ds(0, 96)], ac_send)
    drain(lland.at[pl.ds(0, (C - 1) * CAP_L)], xl_send)
    drain(rland.at[pl.ds(0, (R - 1) * CAP_R)], xr_send)


def sparse_product(blocks, cols, slots, keep):
    tile = (SUB, LANES)
    dma = pltpu.SemaphoreType.DMA
    wide = pltpu.VMEM((AREA, LANES), F32)
    batch = pltpu.VMEM((LANES,) + tile, F32)
    vmem = pl.BlockSpec(memory_space=pltpu.VMEM)
    hbm = pl.BlockSpec(memory_space=pl.ANY)
    return pl.pallas_call(
        kernel,
        out_shape=(
            jax.ShapeDtypeStruct((LANES,) + tile, F32),
            jax.ShapeDtypeStruct((1, 1), F32),
            jax.ShapeDtypeStruct((1, 1), F32),
            jax.ShapeDtypeStruct((LANES,) + tile, F32),
        ),
        in_specs=[hbm, hbm, vmem, vmem],
        out_specs=(vmem, vmem, vmem, hbm),
        scratch_shapes=[
            pltpu.VMEM((C, C) + tile, F32),
            pltpu.VMEM((2 * R * C,) + tile, F32),
            pltpu.VMEM((2 * R * C,) + tile, F32),
            pltpu.VMEM((R * C,) + tile, F32),
            pltpu.VMEM((R, C, LANES), I32),
            pltpu.VMEM((C, R, LANES), I32),
            pltpu.VMEM((C, C, LANES), I32),
            pltpu.VMEM((32, LANES), I32),
            pltpu.SMEM((32, LANES), I32),
            batch, batch, batch,
            wide, wide, wide, wide,
            pltpu.VMEM((R * C - 1, 1, LANES), F32),
            pltpu.VMEM((C * CAP_L,) + tile, F32),
            pltpu.VMEM((R * CAP_R,) + tile, F32),
            pltpu.VMEM((C * CAP_L,) + tile, F32),
            pltpu.VMEM((R * CAP_R,) + tile, F32),
            pltpu.VMEM((LANES, LANES), BF16),
            pltpu.VMEM((1, LANES), F32),
            pltpu.VMEM((C, 1, LANES), F32),
            dma((SUB,)), dma((4 * R,)), dma((6,)), dma, dma,
        ] + [dma] * 18,
        compiler_params=pltpu.CompilerParams(collective_id=0, has_side_effects=True),
    )(blocks, cols, slots, keep)


def dense_product(panel, columns, keep):
    r, c = lax.axis_index("row"), lax.axis_index("col")
    mine = lax.dynamic_slice_in_dim(columns, r * LANES, LANES)
    target = lax.dynamic_slice_in_dim(mine, c, 1, 1)[:, 0]
    far_all = lax.dynamic_slice_in_dim(columns, c, 1, 1)[:, 0]
    flat = panel.reshape(LANES, AREA)

    def around(value, axis):
        size = lax.axis_size(axis)
        return lax.ppermute(value, axis, [((i + 1) % size, i) for i in range(size)])

    def gather(step, carry):
        rights, moving = carry
        rights = lax.dynamic_update_slice_in_dim(rights, moving[None], (r + step) % R, 0)
        return rights, around(moving, "row")

    rights, _ = lax.fori_loop(0, R, gather, (jnp.zeros((R, LANES, AREA), F32), flat))
    rights = rights.reshape(R * LANES, AREA)

    def advance(step, carry):
        totals, left = carry
        m = (c + step) % C
        inner = lax.dynamic_slice_in_dim(mine, m, 1, 1)[:, 0]
        match = (far_all[inner] == target).astype(F32)
        right = rights[inner] * match[:, None]
        term = jnp.einsum(
            "nxz,nzy->nxy", left.reshape(LANES, BS, BS), right.reshape(LANES, BS, BS), precision=HIGHEST
        )
        return totals + term, around(left, "col")

    totals, _ = lax.fori_loop(0, C, advance, (jnp.zeros((LANES, BS, BS), F32), flat))
    ids = r * LANES + jnp.arange(LANES, dtype=I32)
    traces = jnp.trace(totals, axis1=1, axis2=2)
    trace = jnp.full((8, LANES), jnp.sum(jnp.where(target == ids, traces, 0.0)))
    for axis in ("row", "col"):
        def add(step, carry):
            total, moving = carry
            moving = around(moving, axis)
            return total + moving, moving
        trace, _ = lax.fori_loop(1, lax.axis_size(axis), add, (trace, trace))
    filtered = totals.reshape(LANES, AREA) * keep.reshape(LANES, 1).astype(F32)
    return filtered.reshape(LANES, SUB, LANES), trace[0, 0] / (R * LANES)


def shards(blocks, columns, owner_slot, keep_mask):
    keep = keep_mask.T
    filtered, mean, over, panel = sparse_product(blocks, columns.T, owner_slot.reshape(R, LANES), keep)
    filtered, mean = lax.cond(
        over.reshape(()) > 0,
        lambda f, t, s: dense_product(s, columns, keep),
        lambda f, t, s: (f, t),
        filtered, mean.reshape(()), panel,
    )
    return filtered.reshape(LANES, 1, AREA), mean


def solution(mesh):
    in_specs = (P(("row", "col"), None, None), P(), P(), P("row", "col"))
    out_specs = (P("row", "col", None), P())
    return jax.shard_map(shards, mesh=mesh, in_specs=in_specs, out_specs=out_specs, check_vma=False)
```

```python
import functools

import jax
import jax.numpy as jnp
from jax import lax
from jax.experimental import pallas as pl
from jax.experimental.pallas import tpu as pltpu
from jax.sharding import PartitionSpec as P

BS = 32
AREA = BS * BS
SUB, LANES = 8, 128
R, C = 8, 16
HALF = 64
CAP_L = 16
CAP_R = 16
MESH = pl.DeviceIdType.MESH
F32, I32, BF16 = jnp.float32, jnp.int32, jnp.bfloat16
HIGHEST = lax.Precision.HIGHEST


def iota(shape, axis):
    return lax.broadcasted_iota(I32, shape, axis)


def lookup(table, index):
    return jnp.take_along_axis(table, index, axis=1, mode="promise_in_bounds")


def block_products(left, right, out, accumulate):
    def rows(step, carry):
        base = pl.multiple_of(step * (4 * BS), 4 * BS)
        totals = [[None] * 4 for _ in range(4)]
        for z in range(BS):
            tiles = [right[pl.ds(z * BS + 8 * q, 8), :] for q in range(4)]
            for x in range(4):
                factor = jnp.broadcast_to(left[pl.ds(base + x * BS + z, 1), :], (8, LANES))
                for q in range(4):
                    term = factor * tiles[q]
                    totals[x][q] = term if totals[x][q] is None else totals[x][q] + term
        for x in range(4):
            for q in range(4):
                spot = pl.ds(base + x * BS + 8 * q, 8)
                value = totals[x][q]
                out[spot, :] = out[spot, :] + value if accumulate else value
        return carry

    lax.fori_loop(0, BS // 4, rows, 0)


def to_lanes(stacked, out, keep=None):
    for s in range(SUB):
        piece = jnp.transpose(stacked[:, s, :])
        if keep is not None:
            piece = piece * keep
        out[s * LANES : (s + 1) * LANES, :] = piece


def kernel(
    blocks, cols, slots, keep,
    out, mean_out, over_out, panel_out,
    xv, land, agr, dcol, ctb, ct3, tt, lists_v, lists,
    panel, sorted_a, sorted_b, ta, tb, tc, ot,
    lpack, rpack, lland, rland, onehot, tr_row, tr_all,
    in_sem, ct_sem, self_sem, list_sem, out_sem,
    sr_send, sc_send, sr_recv, sc_recv,
    t1_send, t1_recv, ar_send, ac_send, ar_recv, ac_recv, fw_send, fw_recv,
    xl_send, xr_send, xl_recv, xr_recv, yl_send, yl_recv, tr_send, tr_recv, tc_send, tc_recv,
):
    r = lax.axis_index("row")
    c = lax.axis_index("col")
    me = r * C + c
    p, q = c % 2, c // 2
    partner = c + 1 - 2 * p

    def remote(src, dst, send, recv, row, col):
        return pltpu.make_async_remote_copy(
            src_ref=src, dst_ref=dst, send_sem=send, recv_sem=recv,
            device_id=(row, col), device_id_type=MESH,
        )

    def drain(ref, sem):
        pltpu.make_async_copy(ref, ref, sem).wait()

    barrier = pltpu.get_barrier_semaphore()

    def greet(k, carry):
        d = (me + k) % (R * C)
        pl.semaphore_signal(barrier, inc=1, device_id=(d // C, d % C), device_id_type=MESH)
        return carry

    lax.fori_loop(1, R * C, greet, 0)

    loads = [
        pltpu.make_async_copy(blocks.at[:, :, pl.ds(LANES * t, LANES)], xv.at[:, :, t, :], in_sem.at[t])
        for t in range(SUB)
    ]
    for copy in loads:
        copy.start()
    tables = []
    for b in range(R):
        piece = cols.at[:, pl.ds(LANES * b, LANES)]
        tables.append(pltpu.make_async_copy(piece, ctb.at[b], ct_sem.at[4 * b]))
        tables.append(pltpu.make_async_copy(piece, ct3.at[:, b, :], ct_sem.at[4 * b + 1]))
        tables.append(pltpu.make_async_copy(piece, tt.at[:, 2 * b, :], ct_sem.at[4 * b + 2]))
        tables.append(pltpu.make_async_copy(piece, tt.at[:, 2 * b + 1, :], ct_sem.at[4 * b + 3]))
    for copy in tables:
        copy.start()

    for copy in tables:
        copy.wait()
    lane8, lane16 = iota((8, LANES), 1), iota((C, LANES), 1)
    sub8, sub16 = iota((8, LANES), 0), iota((C, LANES), 0)
    def prefix(value, axis):
        place, total, step = iota(value.shape, axis), value, 1
        while step < value.shape[axis]:
            total = total + jnp.where(place >= step, pltpu.roll(total, step, axis), 0)
            step *= 2
        return total - value

    def count_before(flags):
        return prefix(flags.astype(I32), 1)

    def count(flags):
        return jnp.sum(flags.astype(I32), axis=1, keepdims=True)

    own_group = 2 * r + (lane16 // HALF)
    mine = ctb[r]
    target = jnp.broadcast_to(ctb[r, pl.ds(c, 1), :], (C, LANES))
    found = lookup(tt[c], mine % LANES)
    hit = (found == target) & (sub16 != c) & (sub16 != own_group)
    rank = count_before(hit)
    total = jnp.broadcast_to(count(hit), (C, LANES))
    first = prefix(total, 0) + rank
    in_pair = jnp.where(sub16 % 2 == 1, pltpu.roll(total, 1, 0), 0) + rank
    ahead = c - p
    ahead_target = jnp.broadcast_to(ctb[r, pl.ds(ahead, 1), :], (C, LANES))
    ahead_hit = (lookup(tt[ahead], mine % LANES) == ahead_target) & (sub16 != ahead) & (sub16 != own_group)
    in_chip = rank + p * count(ahead_hit)
    spot_a = jnp.minimum(((sub16 % 2) * R + sub16 // 2) * CAP_L + in_chip, C * CAP_L - 1)
    spot_b = jnp.minimum((sub16 // 2) * CAP_R + in_pair, R * CAP_R - 1)
    spots = spot_a + 256 * spot_b
    rows = iota((LANES, LANES), 0)
    chosen = jnp.zeros((LANES, LANES), I32)
    picks = jnp.zeros((LANES, LANES), I32)
    order = jnp.where(hit, first, -1)
    for m in range(C):
        spread = rows == order[m : m + 1, :]
        chosen = jnp.where(spread, 1, chosen)
        picks = jnp.where(spread, spots[m : m + 1, :], picks)
    onehot[...] = chosen.astype(BF16)
    picks = jnp.broadcast_to(jnp.sum(picks, axis=1, keepdims=True), (LANES, LANES))
    picks = jnp.transpose(picks)[0:8, :]

    owner = slots[pl.ds(r, 1), :] // C
    far_owner = lookup(
        jnp.broadcast_to(slots[pl.ds(q, 1), :] // C, (8, LANES)),
        jnp.broadcast_to(ctb[r, pl.ds(c, 1), :] % LANES, (8, LANES)),
    )
    owner8 = jnp.broadcast_to(owner, (8, LANES))
    half = lane8 // HALF
    o_col, o_row = owner8 % C, owner8 // C
    at_land = 2 * owner8 + half
    at_agr = (((o_col % 2) * 4 + (o_col // 2) % 4) * 2 + o_col // 8) * 16 + o_row * 2 + half
    head = jnp.where(sub8 == 0, at_land, jnp.where(sub8 == 1, at_agr, far_owner))
    head = jnp.where(sub8 == 3, picks % 256, jnp.where(sub8 == 4, picks // 256, head))
    lists_v[0:8, :] = head

    left_index = jnp.broadcast_to(ctb[r, pl.ds(c, 1), :] % LANES, (C, LANES))
    left_found = lookup(ctb[q], left_index)
    left_hit = (left_found == mine) & (sub16 != c) & (own_group != c)
    left_rank = count_before(left_hit)
    left_total = jnp.broadcast_to(count(left_hit), (C, LANES))
    left_rank = left_rank + jnp.where(sub16 % 2 == 1, pltpu.roll(left_total, 1, 0), 0)
    at_land16 = jnp.broadcast_to(at_land[0:1, :], (C, LANES))
    left_list = jnp.zeros((C, LANES), I32)
    for k in range(CAP_L):
        value = jnp.sum(jnp.where(left_hit & (left_rank == k), at_land16, 0), axis=1, keepdims=True)
        left_list = jnp.where(lane16 == k, value, left_list)
    left_list = left_list + pltpu.roll(left_list, C - 1, 0)
    lists_v[8:24, :] = left_list

    right_target = ct3[c]
    right_table = jnp.broadcast_to(ct3[c, pl.ds(r, 1), :], (8, LANES))
    their_group = 2 * sub8 + half
    right_list = jnp.zeros((8, LANES), I32)
    flags, places, ranks = [], [], []
    for h in range(2):
        m = 2 * r + h
        place = ct3[m] % LANES
        right_hit = (lookup(right_table, place) == right_target) & (m != c) & (their_group != m)
        right_rank = count_before(right_hit)
        if h == 1:
            right_rank = right_rank + count(flags[0])
        flags.append(right_hit)
        places.append(lookup(at_land, place))
        ranks.append(right_rank)
    for k in range(CAP_R):
        value = sum(
            jnp.sum(jnp.where(flags[h] & (ranks[h] == k), places[h], 0), axis=1, keepdims=True)
            for h in range(2)
        )
        right_list = jnp.where(lane8 == k, value, right_list)
    lists_v[24:32, :] = right_list
    to_smem = pltpu.make_async_copy(lists_v, lists, list_sem)
    to_smem.start()

    for copy in loads:
        copy.wait()
    pl.semaphore_wait(barrier, R * C - 1)

    row_spot = ((p * 4 + q % 4) * 2 + c // 8) * 16 + r * 2
    col_spot = r * C + c

    def row_scatter(k, carry):
        rr, cc = (r + k % R) % R, (c + 8 * (k // R)) % C
        for h in range(2):
            g = 2 * rr + h
            remote(xv.at[g, g], agr.at[row_spot + h], sr_send, sr_recv, rr, cc).start()
        return carry

    lax.fori_loop(1, 2 * R, row_scatter, 0)

    def col_scatter(k, carry):
        g, rr = (c + k % C) % C, r + (k // C) * (1 - 2 * (r % 2))
        remote(xv.at[g, g], dcol.at[col_spot], sc_send, sc_recv, rr, g).start()
        return carry

    lax.fori_loop(1, 2 * C, col_scatter, 0)

    def exchange(k, carry):
        d = (me + k * 37) % (R * C)
        rr, cc = d // C, d % C
        remote(xv.at[pl.ds(2 * rr, 2), cc], land.at[pl.ds(2 * me, 2)], t1_send, t1_recv, rr, cc).start()
        return carry

    lax.fori_loop(1, R * C, exchange, 0)
    own = [
        pltpu.make_async_copy(xv.at[2 * r, 2 * r], agr.at[row_spot], self_sem.at[0]),
        pltpu.make_async_copy(xv.at[2 * r + 1, 2 * r + 1], agr.at[row_spot + 1], self_sem.at[1]),
        pltpu.make_async_copy(xv.at[c, c], dcol.at[r * C + c], self_sem.at[2]),
        pltpu.make_async_copy(xv.at[pl.ds(2 * r, 2), c], land.at[pl.ds(2 * me, 2)], self_sem.at[3]),
    ]
    for copy in own:
        copy.start()

    for copy in own:
        copy.wait()
    piece = agr.at[pl.ds((p * 4 + q % 4) * 32, 32)]
    column_piece = dcol.at[pl.ds((r // 2) * 32, 32)]
    drain(agr.at[pl.ds(0, 30)], sr_recv)
    drain(dcol.at[pl.ds(0, 31)], sc_recv)

    def row_gather(k, carry):
        cc = (c // 8) * 8 + (c % 8 + 2 * k) % 8
        remote(piece, piece, ar_send, ar_recv, r, cc).start()
        return carry

    lax.fori_loop(1, 4, row_gather, 0)

    def col_gather(k, carry):
        remote(column_piece, column_piece, ac_send, ac_recv, (r + 2 * k) % R, c).start()
        return carry

    lax.fori_loop(1, 4, col_gather, 0)

    even = sub16 % 2 == 0
    worst = jnp.full((C, LANES), -1, I32)
    before = jnp.zeros((C, LANES), I32)
    for col in range(C):
        wanted = jnp.broadcast_to(ctb[r, col : col + 1, :], (C, LANES))
        seen = lookup(tt[col], mine % LANES)
        used = jnp.broadcast_to(count((seen == wanted) & (sub16 != col) & (sub16 != own_group)), (C, LANES))
        pair = jnp.where(even, used + pltpu.roll(used, C - 1, 0), 0)
        whole = jnp.sum(used, axis=0, keepdims=True)
        both = used + before if col % 2 else used
        before = used
        worst = jnp.maximum(worst, jnp.maximum(jnp.maximum(both - CAP_L, pair - CAP_R), whole - LANES))
    to_smem.wait()
    drain(land.at[pl.ds(0, 2 * (R * C - 1))], t1_recv)

    def pack_left(d, carry):
        for k in range(CAP_L):
            lpack[d * CAP_L + k] = land[jnp.clip(lists[8 + 2 * d, k], 0, 2 * R * C - 1)]
        return carry

    lax.fori_loop(0, R, pack_left, 0)
    left_spot = pl.ds((p * R + q) * CAP_L, CAP_L)

    def send_left(chip):
        src = lpack.at[pl.ds(chip * CAP_L, CAP_L)]
        remote(src, lland.at[left_spot], xl_send, xl_recv, r, 2 * chip + p).start()

    source = q == r
    pl.when(jnp.logical_not(source))(functools.partial(send_left, r))

    def send_left_rest(k, carry):
        chip = (q + k) % R
        pl.when(chip != r)(functools.partial(send_left, chip))
        return carry

    lax.fori_loop(1, R, send_left_rest, 0)
    keep_left = pltpu.make_async_copy(lpack.at[pl.ds(q * CAP_L, CAP_L)], lland.at[left_spot], self_sem.at[4])
    keep_left.start()

    def pack_right(d, carry):
        for k in range(CAP_R):
            rpack[d * CAP_R + k] = land[jnp.clip(lists[24 + d, k], 0, 2 * R * C - 1)]
        return carry

    lax.fori_loop(0, R, pack_right, 0)
    right_spot = pl.ds(r * CAP_R, CAP_R)

    def send_right(rr):
        src = rpack.at[pl.ds(rr * CAP_R, CAP_R)]
        remote(src, rland.at[right_spot], xr_send, xr_recv, rr, c).start()

    pl.when(jnp.logical_not(source))(functools.partial(send_right, q))

    def send_right_rest(k, carry):
        rr = (r + k) % R
        pl.when(rr != q)(functools.partial(send_right, rr))
        return carry

    lax.fori_loop(1, R, send_right_rest, 0)
    keep_right = pltpu.make_async_copy(rpack.at[right_spot], rland.at[right_spot], self_sem.at[5])
    keep_right.start()

    def collect(i, carry):
        panel[i] = land[jnp.clip(lists[0, i], 0, 2 * R * C - 1)]
        return carry

    lax.fori_loop(0, LANES, collect, 0, unroll=8)

    save = pltpu.make_async_copy(panel, panel_out, out_sem)
    save.start()

    drain(agr.at[pl.ds(0, 96)], ar_recv)
    forward = remote(agr.at[pl.ds(p * 128, 128)], agr.at[pl.ds(p * 128, 128)], fw_send, fw_recv, r, partner)
    forward.start()

    to_lanes(panel, tb)
    drain(dcol.at[pl.ds(0, 96)], ac_recv)

    def collect_column(i, carry):
        sorted_b[i] = dcol[jnp.clip(lists[2, i], 0, R * C - 1)]
        return carry

    lax.fori_loop(0, LANES, collect_column, 0, unroll=8)
    to_lanes(sorted_b, tc)
    block_products(tb, tc, ot, False)
    forward.wait()

    def collect_row(i, carry):
        sorted_a[i] = agr[jnp.clip(lists[1, i], 0, 2 * R * C - 1)]
        return carry

    lax.fori_loop(0, LANES, collect_row, 0, unroll=8)
    lane1 = iota((1, LANES), 1)
    group1 = 2 * r + lane1 // HALF
    to_lanes(sorted_a, ta, (group1 != c).astype(F32))
    block_products(ta, tb, ot, True)

    keep_left.wait()
    drain(lland.at[pl.ds(0, (R - 1) * CAP_L)], xl_recv)
    left_half = lland.at[pl.ds(p * R * CAP_L, R * CAP_L)]
    share = remote(left_half, left_half, yl_send, yl_recv, r, partner)
    share.start()
    keep_right.wait()
    drain(rland.at[pl.ds(0, (R - 1) * CAP_R)], xr_recv)
    share.wait()

    def collect_pairs(i, carry):
        sorted_a[i] = lland[jnp.clip(lists[3, i], 0, C * CAP_L - 1)]
        sorted_b[i] = rland[jnp.clip(lists[4, i], 0, R * CAP_R - 1)]
        return carry

    lax.fori_loop(0, LANES, collect_pairs, 0, unroll=8)
    to_lanes(sorted_a, ta)
    to_lanes(sorted_b, tc)

    @pl.when(source)
    def _():
        diagonal = ot[0:1, :]
        for x in range(1, BS):
            diagonal = diagonal + ot[33 * x : 33 * x + 1, :]
        totals = jnp.zeros((BS, LANES), F32)
        for x in range(BS):
            totals = totals + ta[BS * x : BS * (x + 1), :] * tc[pl.ds(x, BS, stride=BS), :]
        pairs = jnp.sum(totals, axis=0, keepdims=True)
        inside = jnp.broadcast_to((group1 == c).astype(BF16), (8, LANES))
        weight = lax.dot_general(inside, onehot[...], (((1,), (1,)), ((), ())), preferred_element_type=F32)
        partial = jnp.sum(
            jnp.where(group1 == c, diagonal, 0.0) + pairs * weight[0:1, :], axis=1, keepdims=True
        )
        most = jnp.max(jnp.max(worst, axis=0, keepdims=True), axis=1, keepdims=True).astype(F32)
        told = jnp.where(lane1 < HALF, jnp.broadcast_to(partial, (1, LANES)), jnp.broadcast_to(most, (1, LANES)))
        tr_row[p] = told

        def tell(k, carry):
            cc = (c + k) % C
            remote(tr_row.at[p], tr_row.at[p], tr_send, tr_recv, r, cc).start()
            return carry

        lax.fori_loop(1, C, tell, 0)

    block_products(ta, tc, tb, False)

    @pl.when(source)
    def _():
        drain(tr_row.at[pl.ds(0, 1)], tr_recv)
        drain(tr_all.at[pl.ds(0, C - 1)], tr_send)

    @pl.when(jnp.logical_not(source))
    def _():
        drain(tr_row, tr_recv)

    row_spot2 = pl.ds(2 * r, 2)

    def pass_on(k, carry):
        remote(tr_row, tr_all.at[row_spot2], tc_send, tc_recv, (r + k) % R, c).start()
        return carry

    lax.fori_loop(1, R, pass_on, 0)
    spread = onehot[...]
    for s in range(SUB):
        spot = slice(s * LANES, (s + 1) * LANES)
        value = tb[spot, :]
        high = value.astype(BF16)
        rest = value - high.astype(F32)
        middle = rest.astype(BF16)
        low = (rest - middle.astype(F32)).astype(BF16)
        moved = jnp.dot(low, spread, preferred_element_type=F32)
        moved = moved + jnp.dot(middle, spread, preferred_element_type=F32)
        moved = moved + jnp.dot(high, spread, preferred_element_type=F32)
        ot[spot, :] = ot[spot, :] + moved

    kept = keep[...].astype(F32)
    for s in range(SUB):
        spot = slice(s * LANES, (s + 1) * LANES)
        out[:, s, :] = jnp.transpose(ot[spot, :] * kept)

    drain(tr_all.at[pl.ds(0, 2 * (R - 1))], tc_recv)
    drain(tr_all.at[pl.ds(0, 2 * (R - 1))], tc_send)
    tr_all[row_spot2] = tr_row[...]
    trace, most = tr_all[0], tr_all[0]
    for k in range(1, C):
        trace = trace + tr_all[k]
        most = jnp.maximum(most, tr_all[k])
    mean_out[...] = trace[:, 0:1] / (R * LANES)
    over_out[...] = most[:, HALF : HALF + 1]

    save.wait()
    drain(agr.at[pl.ds(0, 30)], sr_send)
    drain(dcol.at[pl.ds(0, 31)], sc_send)
    drain(land.at[pl.ds(0, 2 * (R * C - 1))], t1_send)
    drain(agr.at[pl.ds(0, 96)], ar_send)
    drain(dcol.at[pl.ds(0, 96)], ac_send)
    drain(lland.at[pl.ds(0, (R - 1) * CAP_L)], xl_send)
    drain(rland.at[pl.ds(0, (R - 1) * CAP_R)], xr_send)


def sparse_product(blocks, cols, slots, keep):
    tile = (SUB, LANES)
    dma = pltpu.SemaphoreType.DMA
    wide = pltpu.VMEM((AREA, LANES), F32)
    batch = pltpu.VMEM((LANES,) + tile, F32)
    vmem = pl.BlockSpec(memory_space=pltpu.VMEM)
    hbm = pl.BlockSpec(memory_space=pl.ANY)
    return pl.pallas_call(
        kernel,
        out_shape=(
            jax.ShapeDtypeStruct((LANES,) + tile, F32),
            jax.ShapeDtypeStruct((1, 1), F32),
            jax.ShapeDtypeStruct((1, 1), F32),
            jax.ShapeDtypeStruct((LANES,) + tile, F32),
        ),
        in_specs=[hbm, hbm, vmem, vmem],
        out_specs=(vmem, vmem, vmem, hbm),
        scratch_shapes=[
            pltpu.VMEM((C, C) + tile, F32),
            pltpu.VMEM((2 * R * C,) + tile, F32),
            pltpu.VMEM((2 * R * C,) + tile, F32),
            pltpu.VMEM((R * C,) + tile, F32),
            pltpu.VMEM((R, C, LANES), I32),
            pltpu.VMEM((C, R, LANES), I32),
            pltpu.VMEM((C, C, LANES), I32),
            pltpu.VMEM((32, LANES), I32),
            pltpu.SMEM((32, LANES), I32),
            batch, batch, batch,
            wide, wide, wide, wide,
            pltpu.VMEM((R * CAP_L,) + tile, F32),
            pltpu.VMEM((R * CAP_R,) + tile, F32),
            pltpu.VMEM((C * CAP_L,) + tile, F32),
            pltpu.VMEM((R * CAP_R,) + tile, F32),
            pltpu.VMEM((LANES, LANES), BF16),
            pltpu.VMEM((2, 1, LANES), F32),
            pltpu.VMEM((C, 1, LANES), F32),
            dma((SUB,)), dma((4 * R,)), dma((6,)), dma, dma,
        ] + [dma] * 22,
        compiler_params=pltpu.CompilerParams(collective_id=0, has_side_effects=True),
    )(blocks, cols, slots, keep)


def dense_product(panel, columns, keep):
    r, c = lax.axis_index("row"), lax.axis_index("col")
    mine = lax.dynamic_slice_in_dim(columns, r * LANES, LANES)
    target = lax.dynamic_slice_in_dim(mine, c, 1, 1)[:, 0]
    far_all = lax.dynamic_slice_in_dim(columns, c, 1, 1)[:, 0]
    flat = panel.reshape(LANES, AREA)

    def around(value, axis):
        size = lax.axis_size(axis)
        return lax.ppermute(value, axis, [((i + 1) % size, i) for i in range(size)])

    def gather(step, carry):
        rights, moving = carry
        rights = lax.dynamic_update_slice_in_dim(rights, moving[None], (r + step) % R, 0)
        return rights, around(moving, "row")

    rights, _ = lax.fori_loop(0, R, gather, (jnp.zeros((R, LANES, AREA), F32), flat))
    rights = rights.reshape(R * LANES, AREA)

    def advance(step, carry):
        totals, left = carry
        m = (c + step) % C
        inner = lax.dynamic_slice_in_dim(mine, m, 1, 1)[:, 0]
        match = (far_all[inner] == target).astype(F32)
        right = rights[inner] * match[:, None]
        term = jnp.einsum(
            "nxz,nzy->nxy", left.reshape(LANES, BS, BS), right.reshape(LANES, BS, BS), precision=HIGHEST
        )
        return totals + term, around(left, "col")

    totals, _ = lax.fori_loop(0, C, advance, (jnp.zeros((LANES, BS, BS), F32), flat))
    ids = r * LANES + jnp.arange(LANES, dtype=I32)
    traces = jnp.trace(totals, axis1=1, axis2=2)
    trace = jnp.full((8, LANES), jnp.sum(jnp.where(target == ids, traces, 0.0)))
    for axis in ("row", "col"):
        def add(step, carry):
            total, moving = carry
            moving = around(moving, axis)
            return total + moving, moving
        trace, _ = lax.fori_loop(1, lax.axis_size(axis), add, (trace, trace))
    filtered = totals.reshape(LANES, AREA) * keep.reshape(LANES, 1).astype(F32)
    return filtered.reshape(LANES, SUB, LANES), trace[0, 0] / (R * LANES)


def shards(blocks, columns, owner_slot, keep_mask):
    keep = keep_mask.T
    filtered, mean, over, panel = sparse_product(blocks, columns.T, owner_slot.reshape(R, LANES), keep)
    filtered, mean = lax.cond(
        over.reshape(()) > 0,
        lambda f, t, s: dense_product(s, columns, keep),
        lambda f, t, s: (f, t),
        filtered, mean.reshape(()), panel,
    )
    return filtered.reshape(LANES, 1, AREA), mean


def solution(mesh):
    in_specs = (P(("row", "col"), None, None), P(), P(), P("row", "col"))
    out_specs = (P("row", "col", None), P())
    return jax.shard_map(shards, mesh=mesh, in_specs=in_specs, out_specs=out_specs, check_vma=False)
```

```python
import functools

import jax
import jax.numpy as jnp
from jax import lax
from jax.experimental import pallas as pl
from jax.experimental.pallas import tpu as pltpu
from jax.sharding import PartitionSpec as P

BS = 32
AREA = BS * BS
SUB, LANES = 8, 128
R, C = 8, 16
HALF = 64
CAP_L = 16
CAP_R = 16
MESH = pl.DeviceIdType.MESH
F32, I32, BF16 = jnp.float32, jnp.int32, jnp.bfloat16
HIGHEST = lax.Precision.HIGHEST


def iota(shape, axis):
    return lax.broadcasted_iota(I32, shape, axis)


def lookup(table, index):
    return jnp.take_along_axis(table, index, axis=1, mode="promise_in_bounds")


def block_products(left, right, out, accumulate):
    def rows(step, carry):
        base = pl.multiple_of(step * (4 * BS), 4 * BS)
        totals = [[None] * 4 for _ in range(4)]
        for z in range(BS):
            tiles = [right[pl.ds(z * BS + 8 * q, 8), :] for q in range(4)]
            for x in range(4):
                factor = jnp.broadcast_to(left[pl.ds(base + x * BS + z, 1), :], (8, LANES))
                for q in range(4):
                    term = factor * tiles[q]
                    totals[x][q] = term if totals[x][q] is None else totals[x][q] + term
        for x in range(4):
            for q in range(4):
                spot = pl.ds(base + x * BS + 8 * q, 8)
                value = totals[x][q]
                out[spot, :] = out[spot, :] + value if accumulate else value
        return carry

    lax.fori_loop(0, BS // 4, rows, 0)


def to_lanes(stacked, out, keep=None):
    for s in range(SUB):
        piece = jnp.transpose(stacked[:, s, :])
        if keep is not None:
            piece = piece * keep
        out[s * LANES : (s + 1) * LANES, :] = piece


def kernel(
    blocks, cols, slots, keep,
    out, mean_out, over_out, panel_out,
    xv, land, agr, dcol, ctb, ct3, tt, lists_v, lists,
    panel, sorted_a, sorted_b, pair_a, pair_b, ta, tb, tc, pa, pb, ot,
    lpack, rpack, lland, rland, onehot, tr_row, tr_all,
    in_sem, ct_sem, self_sem, list_sem, out_sem,
    sr_send, sc_send, sr_recv, sc_recv,
    t1_send, t1_recv, ar_send, ac_send, ar_recv, ac_recv, fw_send, fw_recv,
    xl_send, xr_send, xl_recv, xr_recv, yl_send, yl_recv, tr_send, tr_recv, tc_send, tc_recv,
):
    r = lax.axis_index("row")
    c = lax.axis_index("col")
    me = r * C + c
    p, q = c % 2, c // 2
    partner = c + 1 - 2 * p

    def remote(src, dst, send, recv, row, col):
        return pltpu.make_async_remote_copy(
            src_ref=src, dst_ref=dst, send_sem=send, recv_sem=recv,
            device_id=(row, col), device_id_type=MESH,
        )

    def drain(ref, sem):
        pltpu.make_async_copy(ref, ref, sem).wait()

    barrier = pltpu.get_barrier_semaphore()

    def greet(k, carry):
        d = (me + k) % (R * C)
        pl.semaphore_signal(barrier, inc=1, device_id=(d // C, d % C), device_id_type=MESH)
        return carry

    lax.fori_loop(1, R * C, greet, 0)

    loads = [
        pltpu.make_async_copy(blocks.at[:, :, pl.ds(LANES * t, LANES)], xv.at[:, :, t, :], in_sem.at[t])
        for t in range(SUB)
    ]
    for copy in loads:
        copy.start()
    tables = []
    for b in range(R):
        piece = cols.at[:, pl.ds(LANES * b, LANES)]
        tables.append(pltpu.make_async_copy(piece, ctb.at[b], ct_sem.at[4 * b]))
        tables.append(pltpu.make_async_copy(piece, ct3.at[:, b, :], ct_sem.at[4 * b + 1]))
        tables.append(pltpu.make_async_copy(piece, tt.at[:, 2 * b, :], ct_sem.at[4 * b + 2]))
        tables.append(pltpu.make_async_copy(piece, tt.at[:, 2 * b + 1, :], ct_sem.at[4 * b + 3]))
    for copy in tables:
        copy.start()

    for copy in tables:
        copy.wait()
    lane8, lane16 = iota((8, LANES), 1), iota((C, LANES), 1)
    sub8, sub16 = iota((8, LANES), 0), iota((C, LANES), 0)
    def prefix(value, axis):
        place, total, step = iota(value.shape, axis), value, 1
        while step < value.shape[axis]:
            total = total + jnp.where(place >= step, pltpu.roll(total, step, axis), 0)
            step *= 2
        return total - value

    def count_before(flags):
        return prefix(flags.astype(I32), 1)

    def count(flags):
        return jnp.sum(flags.astype(I32), axis=1, keepdims=True)

    own_group = 2 * r + (lane16 // HALF)
    mine = ctb[r]
    target = jnp.broadcast_to(ctb[r, pl.ds(c, 1), :], (C, LANES))
    found = lookup(tt[c], mine % LANES)
    hit = (found == target) & (sub16 != c) & (sub16 != own_group)
    rank = count_before(hit)
    total = jnp.broadcast_to(count(hit), (C, LANES))
    first = prefix(total, 0) + rank
    in_pair = jnp.where(sub16 % 2 == 1, pltpu.roll(total, 1, 0), 0) + rank
    ahead = c - p
    ahead_target = jnp.broadcast_to(ctb[r, pl.ds(ahead, 1), :], (C, LANES))
    ahead_hit = (lookup(tt[ahead], mine % LANES) == ahead_target) & (sub16 != ahead) & (sub16 != own_group)
    in_chip = rank + p * count(ahead_hit)
    spot_a = jnp.minimum(((sub16 % 2) * R + sub16 // 2) * CAP_L + in_chip, C * CAP_L - 1)
    spot_b = jnp.minimum((sub16 // 2) * CAP_R + in_pair, R * CAP_R - 1)
    spots = spot_a + 256 * spot_b
    rows = iota((LANES, LANES), 0)
    chosen = jnp.zeros((LANES, LANES), I32)
    picks = jnp.zeros((LANES, LANES), I32)
    order = jnp.where(hit, first, -1)
    for m in range(C):
        spread = rows == order[m : m + 1, :]
        chosen = jnp.where(spread, 1, chosen)
        picks = jnp.where(spread, spots[m : m + 1, :], picks)
    onehot[...] = chosen.astype(BF16)
    picks = jnp.broadcast_to(jnp.sum(picks, axis=1, keepdims=True), (LANES, LANES))
    picks = jnp.transpose(picks)[0:8, :]

    owner = slots[pl.ds(r, 1), :] // C
    far_owner = lookup(
        jnp.broadcast_to(slots[pl.ds(q, 1), :] // C, (8, LANES)),
        jnp.broadcast_to(ctb[r, pl.ds(c, 1), :] % LANES, (8, LANES)),
    )
    owner8 = jnp.broadcast_to(owner, (8, LANES))
    half = lane8 // HALF
    o_col, o_row = owner8 % C, owner8 // C
    at_land = 2 * owner8 + half
    at_agr = (((o_col % 2) * 4 + (o_col // 2) % 4) * 2 + o_col // 8) * 16 + o_row * 2 + half
    head = jnp.where(sub8 == 0, at_land, jnp.where(sub8 == 1, at_agr, far_owner))
    head = jnp.where(sub8 == 3, picks % 256, jnp.where(sub8 == 4, picks // 256, head))
    lists_v[0:8, :] = head

    left_index = jnp.broadcast_to(ctb[r, pl.ds(c, 1), :] % LANES, (C, LANES))
    left_found = lookup(ctb[q], left_index)
    left_hit = (left_found == mine) & (sub16 != c) & (own_group != c)
    left_rank = count_before(left_hit)
    left_total = jnp.broadcast_to(count(left_hit), (C, LANES))
    left_rank = left_rank + jnp.where(sub16 % 2 == 1, pltpu.roll(left_total, 1, 0), 0)
    at_land16 = jnp.broadcast_to(at_land[0:1, :], (C, LANES))
    left_list = jnp.zeros((C, LANES), I32)
    for k in range(CAP_L):
        value = jnp.sum(jnp.where(left_hit & (left_rank == k), at_land16, 0), axis=1, keepdims=True)
        left_list = jnp.where(lane16 == k, value, left_list)
    left_list = left_list + pltpu.roll(left_list, C - 1, 0)
    lists_v[8:24, :] = left_list

    right_target = ct3[c]
    right_table = jnp.broadcast_to(ct3[c, pl.ds(r, 1), :], (8, LANES))
    their_group = 2 * sub8 + half
    right_list = jnp.zeros((8, LANES), I32)
    flags, places, ranks = [], [], []
    for h in range(2):
        m = 2 * r + h
        place = ct3[m] % LANES
        right_hit = (lookup(right_table, place) == right_target) & (m != c) & (their_group != m)
        right_rank = count_before(right_hit)
        if h == 1:
            right_rank = right_rank + count(flags[0])
        flags.append(right_hit)
        places.append(lookup(at_land, place))
        ranks.append(right_rank)
    for k in range(CAP_R):
        value = sum(
            jnp.sum(jnp.where(flags[h] & (ranks[h] == k), places[h], 0), axis=1, keepdims=True)
            for h in range(2)
        )
        right_list = jnp.where(lane8 == k, value, right_list)
    lists_v[24:32, :] = right_list
    to_smem = pltpu.make_async_copy(lists_v, lists, list_sem)
    to_smem.start()

    for copy in loads:
        copy.wait()
    pl.semaphore_wait(barrier, R * C - 1)

    row_spot = ((p * 4 + q % 4) * 2 + c // 8) * 16 + r * 2
    col_spot = r * C + c

    def row_scatter(k, carry):
        rr, cc = (r + k % R) % R, (c + 8 * (k // R)) % C
        for h in range(2):
            g = 2 * rr + h
            remote(xv.at[g, g], agr.at[row_spot + h], sr_send, sr_recv, rr, cc).start()
        return carry

    lax.fori_loop(1, 2 * R, row_scatter, 0)

    def col_scatter(k, carry):
        g, rr = (c + k % C) % C, r + (k // C) * (1 - 2 * (r % 2))
        remote(xv.at[g, g], dcol.at[col_spot], sc_send, sc_recv, rr, g).start()
        return carry

    lax.fori_loop(1, 2 * C, col_scatter, 0)

    def exchange(k, carry):
        d = (me + k * 37) % (R * C)
        rr, cc = d // C, d % C
        remote(xv.at[pl.ds(2 * rr, 2), cc], land.at[pl.ds(2 * me, 2)], t1_send, t1_recv, rr, cc).start()
        return carry

    lax.fori_loop(1, R * C, exchange, 0)
    own = [
        pltpu.make_async_copy(xv.at[2 * r, 2 * r], agr.at[row_spot], self_sem.at[0]),
        pltpu.make_async_copy(xv.at[2 * r + 1, 2 * r + 1], agr.at[row_spot + 1], self_sem.at[1]),
        pltpu.make_async_copy(xv.at[c, c], dcol.at[r * C + c], self_sem.at[2]),
        pltpu.make_async_copy(xv.at[pl.ds(2 * r, 2), c], land.at[pl.ds(2 * me, 2)], self_sem.at[3]),
    ]
    for copy in own:
        copy.start()

    for copy in own:
        copy.wait()
    piece = agr.at[pl.ds((p * 4 + q % 4) * 32, 32)]
    column_piece = dcol.at[pl.ds((r // 2) * 32, 32)]
    drain(agr.at[pl.ds(0, 30)], sr_recv)
    drain(dcol.at[pl.ds(0, 31)], sc_recv)

    def row_gather(k, carry):
        cc = (c // 8) * 8 + (c % 8 + 2 * k) % 8
        remote(piece, piece, ar_send, ar_recv, r, cc).start()
        return carry

    lax.fori_loop(1, 4, row_gather, 0)

    def col_gather(k, carry):
        remote(column_piece, column_piece, ac_send, ac_recv, (r + 2 * k) % R, c).start()
        return carry

    lax.fori_loop(1, 4, col_gather, 0)

    even = sub16 % 2 == 0
    worst = jnp.full((C, LANES), -1, I32)
    before = jnp.zeros((C, LANES), I32)
    for col in range(C):
        wanted = jnp.broadcast_to(ctb[r, col : col + 1, :], (C, LANES))
        seen = lookup(tt[col], mine % LANES)
        used = jnp.broadcast_to(count((seen == wanted) & (sub16 != col) & (sub16 != own_group)), (C, LANES))
        pair = jnp.where(even, used + pltpu.roll(used, C - 1, 0), 0)
        whole = jnp.sum(used, axis=0, keepdims=True)
        both = used + before if col % 2 else used
        before = used
        worst = jnp.maximum(worst, jnp.maximum(jnp.maximum(both - CAP_L, pair - CAP_R), whole - LANES))
    to_smem.wait()
    drain(land.at[pl.ds(0, 2 * (R * C - 1))], t1_recv)

    def pack_left(d, carry):
        for k in range(CAP_L):
            lpack[d * CAP_L + k] = land[jnp.clip(lists[8 + 2 * d, k], 0, 2 * R * C - 1)]
        return carry

    lax.fori_loop(0, R, pack_left, 0)
    def pack_right(d, carry):
        for k in range(CAP_R):
            rpack[d * CAP_R + k] = land[jnp.clip(lists[24 + d, k], 0, 2 * R * C - 1)]
        return carry

    lax.fori_loop(0, R, pack_right, 0)
    left_spot = pl.ds((p * R + q) * CAP_L, CAP_L)

    def send_left(chip):
        src = lpack.at[pl.ds(chip * CAP_L, CAP_L)]
        remote(src, lland.at[left_spot], xl_send, xl_recv, r, 2 * chip + p).start()

    right_spot = pl.ds(r * CAP_R, CAP_R)

    def send_right(rr):
        src = rpack.at[pl.ds(rr * CAP_R, CAP_R)]
        remote(src, rland.at[right_spot], xr_send, xr_recv, rr, c).start()

    source = q == r
    pl.when(jnp.logical_not(source))(functools.partial(send_left, r))
    pl.when(jnp.logical_not(source))(functools.partial(send_right, q))

    def send_left_rest(k, carry):
        chip = (q + k) % R
        pl.when(chip != r)(functools.partial(send_left, chip))
        return carry

    lax.fori_loop(1, R, send_left_rest, 0)
    keep_left = pltpu.make_async_copy(lpack.at[pl.ds(q * CAP_L, CAP_L)], lland.at[left_spot], self_sem.at[4])
    keep_left.start()

    def send_right_rest(k, carry):
        rr = (r + k) % R
        pl.when(rr != q)(functools.partial(send_right, rr))
        return carry

    lax.fori_loop(1, R, send_right_rest, 0)
    keep_right = pltpu.make_async_copy(rpack.at[right_spot], rland.at[right_spot], self_sem.at[5])
    keep_right.start()

    def collect(i, carry):
        panel[i] = land[jnp.clip(lists[0, i], 0, 2 * R * C - 1)]
        return carry

    lax.fori_loop(0, LANES, collect, 0, unroll=8)

    save = pltpu.make_async_copy(panel, panel_out, out_sem)
    save.start()

    drain(agr.at[pl.ds(0, 96)], ar_recv)
    forward = remote(agr.at[pl.ds(p * 128, 128)], agr.at[pl.ds(p * 128, 128)], fw_send, fw_recv, r, partner)
    forward.start()

    to_lanes(panel, tb)
    lane1 = iota((1, LANES), 1)
    group1 = 2 * r + lane1 // HALF

    def receive_pairs():
        keep_left.wait()
        drain(lland.at[pl.ds(0, (R - 1) * CAP_L)], xl_recv)
        left_half = lland.at[pl.ds(p * R * CAP_L, R * CAP_L)]
        share = remote(left_half, left_half, yl_send, yl_recv, r, partner)
        share.start()
        keep_right.wait()
        drain(rland.at[pl.ds(0, (R - 1) * CAP_R)], xr_recv)
        share.wait()

        def collect_pairs(i, carry):
            pair_a[i] = lland[jnp.clip(lists[3, i], 0, C * CAP_L - 1)]
            pair_b[i] = rland[jnp.clip(lists[4, i], 0, R * CAP_R - 1)]
            return carry

        lax.fori_loop(0, LANES, collect_pairs, 0, unroll=8)
        to_lanes(pair_a, pa)
        to_lanes(pair_b, pb)

    @pl.when(source)
    def _():
        receive_pairs()
        own_terms, totals = jnp.zeros((BS, LANES), F32), jnp.zeros((BS, LANES), F32)
        for x in range(BS):
            own_terms = own_terms + tb[BS * x : BS * (x + 1), :] * tb[pl.ds(x, BS, stride=BS), :]
            totals = totals + pa[BS * x : BS * (x + 1), :] * pb[pl.ds(x, BS, stride=BS), :]
        diagonal = jnp.sum(own_terms, axis=0, keepdims=True)
        pairs = jnp.sum(totals, axis=0, keepdims=True)
        inside = jnp.broadcast_to((group1 == c).astype(BF16), (8, LANES))
        weight = lax.dot_general(inside, onehot[...], (((1,), (1,)), ((), ())), preferred_element_type=F32)
        partial = jnp.sum(
            jnp.where(group1 == c, diagonal, 0.0) + pairs * weight[0:1, :], axis=1, keepdims=True
        )
        most = jnp.max(jnp.max(worst, axis=0, keepdims=True), axis=1, keepdims=True).astype(F32)
        told = jnp.where(lane1 < HALF, jnp.broadcast_to(partial, (1, LANES)), jnp.broadcast_to(most, (1, LANES)))
        tr_row[p] = told

        def tell(k, carry):
            cc = (c + k) % C
            remote(tr_row.at[p], tr_row.at[p], tr_send, tr_recv, r, cc).start()
            return carry

        lax.fori_loop(1, C, tell, 0)

    drain(dcol.at[pl.ds(0, 96)], ac_recv)

    def collect_column(i, carry):
        sorted_b[i] = dcol[jnp.clip(lists[2, i], 0, R * C - 1)]
        return carry

    lax.fori_loop(0, LANES, collect_column, 0, unroll=8)
    to_lanes(sorted_b, tc)
    block_products(tb, tc, ot, False)
    forward.wait()

    def collect_row(i, carry):
        sorted_a[i] = agr[jnp.clip(lists[1, i], 0, 2 * R * C - 1)]
        return carry

    lax.fori_loop(0, LANES, collect_row, 0, unroll=8)
    to_lanes(sorted_a, ta, (group1 != c).astype(F32))
    block_products(ta, tb, ot, True)

    @pl.when(source)
    def _():
        drain(tr_row.at[pl.ds(0, 1)], tr_recv)
        drain(tr_all.at[pl.ds(0, C - 1)], tr_send)

    @pl.when(jnp.logical_not(source))
    def _():
        drain(tr_row, tr_recv)

    row_spot2 = pl.ds(2 * r, 2)

    def pass_on(k, carry):
        remote(tr_row, tr_all.at[row_spot2], tc_send, tc_recv, (r + k) % R, c).start()
        return carry

    lax.fori_loop(1, R, pass_on, 0)

    pl.when(jnp.logical_not(source))(receive_pairs)

    block_products(pa, pb, tb, False)

    spread = onehot[...]
    for s in range(SUB):
        spot = slice(s * LANES, (s + 1) * LANES)
        value = tb[spot, :]
        high = value.astype(BF16)
        rest = value - high.astype(F32)
        middle = rest.astype(BF16)
        low = (rest - middle.astype(F32)).astype(BF16)
        moved = jnp.dot(low, spread, preferred_element_type=F32)
        moved = moved + jnp.dot(middle, spread, preferred_element_type=F32)
        moved = moved + jnp.dot(high, spread, preferred_element_type=F32)
        ot[spot, :] = ot[spot, :] + moved

    kept = keep[...].astype(F32)
    for s in range(SUB):
        spot = slice(s * LANES, (s + 1) * LANES)
        out[:, s, :] = jnp.transpose(ot[spot, :] * kept)

    drain(tr_all.at[pl.ds(0, 2 * (R - 1))], tc_recv)
    drain(tr_all.at[pl.ds(0, 2 * (R - 1))], tc_send)
    tr_all[row_spot2] = tr_row[...]
    trace, most = tr_all[0], tr_all[0]
    for k in range(1, C):
        trace = trace + tr_all[k]
        most = jnp.maximum(most, tr_all[k])
    mean_out[...] = trace[:, 0:1] / (R * LANES)
    over_out[...] = most[:, HALF : HALF + 1]

    save.wait()
    drain(agr.at[pl.ds(0, 30)], sr_send)
    drain(dcol.at[pl.ds(0, 31)], sc_send)
    drain(land.at[pl.ds(0, 2 * (R * C - 1))], t1_send)
    drain(agr.at[pl.ds(0, 96)], ar_send)
    drain(dcol.at[pl.ds(0, 96)], ac_send)
    drain(lland.at[pl.ds(0, (R - 1) * CAP_L)], xl_send)
    drain(rland.at[pl.ds(0, (R - 1) * CAP_R)], xr_send)


def sparse_product(blocks, cols, slots, keep):
    tile = (SUB, LANES)
    dma = pltpu.SemaphoreType.DMA
    wide = pltpu.VMEM((AREA, LANES), F32)
    batch = pltpu.VMEM((LANES,) + tile, F32)
    vmem = pl.BlockSpec(memory_space=pltpu.VMEM)
    hbm = pl.BlockSpec(memory_space=pl.ANY)
    return pl.pallas_call(
        kernel,
        out_shape=(
            jax.ShapeDtypeStruct((LANES,) + tile, F32),
            jax.ShapeDtypeStruct((1, 1), F32),
            jax.ShapeDtypeStruct((1, 1), F32),
            jax.ShapeDtypeStruct((LANES,) + tile, F32),
        ),
        in_specs=[hbm, hbm, vmem, vmem],
        out_specs=(vmem, vmem, vmem, hbm),
        scratch_shapes=[
            pltpu.VMEM((C, C) + tile, F32),
            pltpu.VMEM((2 * R * C,) + tile, F32),
            pltpu.VMEM((2 * R * C,) + tile, F32),
            pltpu.VMEM((R * C,) + tile, F32),
            pltpu.VMEM((R, C, LANES), I32),
            pltpu.VMEM((C, R, LANES), I32),
            pltpu.VMEM((C, C, LANES), I32),
            pltpu.VMEM((32, LANES), I32),
            pltpu.SMEM((32, LANES), I32),
            batch, batch, batch, batch, batch,
            wide, wide, wide, wide, wide, wide,
            pltpu.VMEM((R * CAP_L,) + tile, F32),
            pltpu.VMEM((R * CAP_R,) + tile, F32),
            pltpu.VMEM((C * CAP_L,) + tile, F32),
            pltpu.VMEM((R * CAP_R,) + tile, F32),
            pltpu.VMEM((LANES, LANES), BF16),
            pltpu.VMEM((2, 1, LANES), F32),
            pltpu.VMEM((C, 1, LANES), F32),
            dma((SUB,)), dma((4 * R,)), dma((6,)), dma, dma,
        ] + [dma] * 22,
        compiler_params=pltpu.CompilerParams(collective_id=0, has_side_effects=True),
    )(blocks, cols, slots, keep)


def dense_product(panel, columns, keep):
    r, c = lax.axis_index("row"), lax.axis_index("col")
    mine = lax.dynamic_slice_in_dim(columns, r * LANES, LANES)
    target = lax.dynamic_slice_in_dim(mine, c, 1, 1)[:, 0]
    far_all = lax.dynamic_slice_in_dim(columns, c, 1, 1)[:, 0]
    flat = panel.reshape(LANES, AREA)

    def around(value, axis):
        size = lax.axis_size(axis)
        return lax.ppermute(value, axis, [((i + 1) % size, i) for i in range(size)])

    def gather(step, carry):
        rights, moving = carry
        rights = lax.dynamic_update_slice_in_dim(rights, moving[None], (r + step) % R, 0)
        return rights, around(moving, "row")

    rights, _ = lax.fori_loop(0, R, gather, (jnp.zeros((R, LANES, AREA), F32), flat))
    rights = rights.reshape(R * LANES, AREA)

    def advance(step, carry):
        totals, left = carry
        m = (c + step) % C
        inner = lax.dynamic_slice_in_dim(mine, m, 1, 1)[:, 0]
        match = (far_all[inner] == target).astype(F32)
        right = rights[inner] * match[:, None]
        term = jnp.einsum(
            "nxz,nzy->nxy", left.reshape(LANES, BS, BS), right.reshape(LANES, BS, BS), precision=HIGHEST
        )
        return totals + term, around(left, "col")

    totals, _ = lax.fori_loop(0, C, advance, (jnp.zeros((LANES, BS, BS), F32), flat))
    ids = r * LANES + jnp.arange(LANES, dtype=I32)
    traces = jnp.trace(totals, axis1=1, axis2=2)
    trace = jnp.full((8, LANES), jnp.sum(jnp.where(target == ids, traces, 0.0)))
    for axis in ("row", "col"):
        def add(step, carry):
            total, moving = carry
            moving = around(moving, axis)
            return total + moving, moving
        trace, _ = lax.fori_loop(1, lax.axis_size(axis), add, (trace, trace))
    filtered = totals.reshape(LANES, AREA) * keep.reshape(LANES, 1).astype(F32)
    filtered = lax.optimization_barrier(filtered.reshape(SUB * LANES, LANES))
    return filtered, trace[0, 0] / (R * LANES)


def shards(blocks, columns, owner_slot, keep_mask):
    keep = keep_mask.T
    filtered, mean, over, panel = sparse_product(blocks, columns.T, owner_slot.reshape(R, LANES), keep)
    filtered, mean = lax.cond(
        over.reshape(()) > 0,
        lambda f, t, s: dense_product(s, columns, keep),
        lambda f, t, s: (f, t),
        filtered.reshape(SUB * LANES, LANES), mean.reshape(()), panel,
    )
    filtered = lax.optimization_barrier(filtered)
    return filtered.reshape(LANES, 1, AREA), mean


def solution(mesh):
    in_specs = (P(("row", "col"), None, None), P(), P(), P("row", "col"))
    out_specs = (P("row", "col", None), P())
    return jax.shard_map(shards, mesh=mesh, in_specs=in_specs, out_specs=out_specs, check_vma=False)
```

```python
import functools

import jax
import jax.numpy as jnp
from jax import lax
from jax.experimental import pallas as pl
from jax.experimental.pallas import tpu as pltpu
from jax.sharding import PartitionSpec as P

BS = 32
AREA = BS * BS
SUB, LANES = 8, 128
R, C = 8, 16
HALF = 64
CAP_L = 16
CAP_R = 16
MESH = pl.DeviceIdType.MESH
F32, I32, BF16 = jnp.float32, jnp.int32, jnp.bfloat16
HIGHEST = lax.Precision.HIGHEST


def iota(shape, axis):
    return lax.broadcasted_iota(I32, shape, axis)


def lookup(table, index):
    return jnp.take_along_axis(table, index, axis=1, mode="promise_in_bounds")


def block_products(left, right, out, accumulate):
    def rows(step, carry):
        base = pl.multiple_of(step * (4 * BS), 4 * BS)
        totals = [[None] * 4 for _ in range(4)]
        for z in range(BS):
            tiles = [right[pl.ds(z * BS + 8 * q, 8), :] for q in range(4)]
            for x in range(4):
                factor = jnp.broadcast_to(left[pl.ds(base + x * BS + z, 1), :], (8, LANES))
                for q in range(4):
                    term = factor * tiles[q]
                    totals[x][q] = term if totals[x][q] is None else totals[x][q] + term
        for x in range(4):
            for q in range(4):
                spot = pl.ds(base + x * BS + 8 * q, 8)
                value = totals[x][q]
                out[spot, :] = out[spot, :] + value if accumulate else value
        return carry

    lax.fori_loop(0, BS // 4, rows, 0)


def to_lanes(stacked, out, keep=None):
    for s in range(SUB):
        piece = jnp.transpose(stacked[:, s, :])
        if keep is not None:
            piece = piece * keep
        out[s * LANES : (s + 1) * LANES, :] = piece


def kernel(
    blocks, cols, slots, keep,
    out, mean_out, over_out, panel_out,
    xv, land, agr, dcol, ctb, ct3, tt, lists_v, lists,
    panel, sorted_a, sorted_b, pair_a, pair_b, ta, tb, tc, pa, pb, ot,
    lpack, rpack, lland, rland, onehot, tr_row, tr_all,
    in_sem, ct_sem, self_sem, list_sem, out_sem,
    sr_send, sc_send, sr_recv, sc_recv,
    t1_send, t1_recv, ar_send, ac_send, ar_recv, ac_recv, fw_send, fw_recv,
    xl_send, xr_send, xl_recv, xr_recv, yl_send, yl_recv, tr_send, tr_recv, tc_send, tc_recv,
):
    r = lax.axis_index("row")
    c = lax.axis_index("col")
    me = r * C + c
    p, q = c % 2, c // 2
    partner = c + 1 - 2 * p

    def remote(src, dst, send, recv, row, col):
        return pltpu.make_async_remote_copy(
            src_ref=src, dst_ref=dst, send_sem=send, recv_sem=recv,
            device_id=(row, col), device_id_type=MESH,
        )

    def drain(ref, sem):
        pltpu.make_async_copy(ref, ref, sem).wait()

    barrier = pltpu.get_barrier_semaphore()

    def greet(k, carry):
        d = (me + k) % (R * C)
        pl.semaphore_signal(barrier, inc=1, device_id=(d // C, d % C), device_id_type=MESH)
        return carry

    lax.fori_loop(1, R * C, greet, 0)

    loads = [
        pltpu.make_async_copy(blocks.at[:, :, pl.ds(LANES * t, LANES)], xv.at[:, :, t, :], in_sem.at[t])
        for t in range(SUB)
    ]
    for copy in loads:
        copy.start()
    tables = []
    for b in range(R):
        piece = cols.at[:, pl.ds(LANES * b, LANES)]
        tables.append(pltpu.make_async_copy(piece, ctb.at[b], ct_sem.at[4 * b]))
        tables.append(pltpu.make_async_copy(piece, ct3.at[:, b, :], ct_sem.at[4 * b + 1]))
        tables.append(pltpu.make_async_copy(piece, tt.at[:, 2 * b, :], ct_sem.at[4 * b + 2]))
        tables.append(pltpu.make_async_copy(piece, tt.at[:, 2 * b + 1, :], ct_sem.at[4 * b + 3]))
    for copy in tables:
        copy.start()

    for copy in tables:
        copy.wait()
    lane8, lane16 = iota((8, LANES), 1), iota((C, LANES), 1)
    sub8, sub16 = iota((8, LANES), 0), iota((C, LANES), 0)
    def prefix(value, axis):
        place, total, step = iota(value.shape, axis), value, 1
        while step < value.shape[axis]:
            total = total + jnp.where(place >= step, pltpu.roll(total, step, axis), 0)
            step *= 2
        return total - value

    def count_before(flags):
        return prefix(flags.astype(I32), 1)

    def count(flags):
        return jnp.sum(flags.astype(I32), axis=1, keepdims=True)

    own_group = 2 * r + (lane16 // HALF)
    mine = ctb[r]
    target = jnp.broadcast_to(ctb[r, pl.ds(c, 1), :], (C, LANES))
    found = lookup(tt[c], mine % LANES)
    hit = (found == target) & (sub16 != c) & (sub16 != own_group)
    rank = count_before(hit)
    total = jnp.broadcast_to(count(hit), (C, LANES))
    first = prefix(total, 0) + rank
    in_pair = jnp.where(sub16 % 2 == 1, pltpu.roll(total, 1, 0), 0) + rank
    ahead = c - p
    ahead_target = jnp.broadcast_to(ctb[r, pl.ds(ahead, 1), :], (C, LANES))
    ahead_hit = (lookup(tt[ahead], mine % LANES) == ahead_target) & (sub16 != ahead) & (sub16 != own_group)
    in_chip = rank + p * count(ahead_hit)
    spot_a = jnp.minimum(((sub16 % 2) * R + sub16 // 2) * CAP_L + in_chip, C * CAP_L - 1)
    spot_b = jnp.minimum((sub16 // 2) * CAP_R + in_pair, R * CAP_R - 1)
    spots = spot_a + 256 * spot_b
    rows = iota((LANES, LANES), 0)
    chosen = jnp.zeros((LANES, LANES), I32)
    picks = jnp.zeros((LANES, LANES), I32)
    order = jnp.where(hit, first, -1)
    for m in range(C):
        spread = rows == order[m : m + 1, :]
        chosen = jnp.where(spread, 1, chosen)
        picks = jnp.where(spread, spots[m : m + 1, :], picks)
    onehot[...] = chosen.astype(BF16)
    picks = jnp.broadcast_to(jnp.sum(picks, axis=1, keepdims=True), (LANES, LANES))
    picks = jnp.transpose(picks)[0:8, :]

    owner = slots[pl.ds(r, 1), :] // C
    far_owner = lookup(
        jnp.broadcast_to(slots[pl.ds(q, 1), :] // C, (8, LANES)),
        jnp.broadcast_to(ctb[r, pl.ds(c, 1), :] % LANES, (8, LANES)),
    )
    owner8 = jnp.broadcast_to(owner, (8, LANES))
    half = lane8 // HALF
    o_col, o_row = owner8 % C, owner8 // C
    at_land = 2 * owner8 + half
    at_agr = (((o_col % 2) * 4 + (o_col // 2) % 4) * 2 + o_col // 8) * 16 + o_row * 2 + half
    head = jnp.where(sub8 == 0, at_land, jnp.where(sub8 == 1, at_agr, far_owner))
    head = jnp.where(sub8 == 3, picks % 256, jnp.where(sub8 == 4, picks // 256, head))
    lists_v[0:8, :] = head

    left_index = jnp.broadcast_to(ctb[r, pl.ds(c, 1), :] % LANES, (C, LANES))
    left_found = lookup(ctb[q], left_index)
    left_hit = (left_found == mine) & (sub16 != c) & (own_group != c)
    left_rank = count_before(left_hit)
    left_total = jnp.broadcast_to(count(left_hit), (C, LANES))
    left_rank = left_rank + jnp.where(sub16 % 2 == 1, pltpu.roll(left_total, 1, 0), 0)
    at_land16 = jnp.broadcast_to(at_land[0:1, :], (C, LANES))
    left_list = jnp.zeros((C, LANES), I32)
    for k in range(CAP_L):
        value = jnp.sum(jnp.where(left_hit & (left_rank == k), at_land16, 0), axis=1, keepdims=True)
        left_list = jnp.where(lane16 == k, value, left_list)
    left_list = left_list + pltpu.roll(left_list, C - 1, 0)
    lists_v[8:24, :] = left_list

    right_target = ct3[c]
    right_table = jnp.broadcast_to(ct3[c, pl.ds(r, 1), :], (8, LANES))
    their_group = 2 * sub8 + half
    right_list = jnp.zeros((8, LANES), I32)
    flags, places, ranks = [], [], []
    for h in range(2):
        m = 2 * r + h
        place = ct3[m] % LANES
        right_hit = (lookup(right_table, place) == right_target) & (m != c) & (their_group != m)
        right_rank = count_before(right_hit)
        if h == 1:
            right_rank = right_rank + count(flags[0])
        flags.append(right_hit)
        places.append(lookup(at_land, place))
        ranks.append(right_rank)
    for k in range(CAP_R):
        value = sum(
            jnp.sum(jnp.where(flags[h] & (ranks[h] == k), places[h], 0), axis=1, keepdims=True)
            for h in range(2)
        )
        right_list = jnp.where(lane8 == k, value, right_list)
    lists_v[24:32, :] = right_list
    to_smem = pltpu.make_async_copy(lists_v, lists, list_sem)
    to_smem.start()

    for copy in loads:
        copy.wait()
    pl.semaphore_wait(barrier, R * C - 1)

    row_spot = ((p * 4 + q % 4) * 2 + c // 8) * 16 + r * 2
    col_spot = r * C + c

    def row_scatter(k, carry):
        rr, cc = (r + k % R) % R, (c + 8 * (k // R)) % C
        for h in range(2):
            g = 2 * rr + h
            remote(xv.at[g, g], agr.at[row_spot + h], sr_send, sr_recv, rr, cc).start()
        return carry

    lax.fori_loop(1, 2 * R, row_scatter, 0)

    def col_scatter(k, carry):
        g, rr = (c + k % C) % C, r + (k // C) * (1 - 2 * (r % 2))
        remote(xv.at[g, g], dcol.at[col_spot], sc_send, sc_recv, rr, g).start()
        return carry

    lax.fori_loop(1, 2 * C, col_scatter, 0)

    def exchange(k, carry):
        d = (me + k * 37) % (R * C)
        rr, cc = d // C, d % C
        remote(xv.at[pl.ds(2 * rr, 2), cc], land.at[pl.ds(2 * me, 2)], t1_send, t1_recv, rr, cc).start()
        return carry

    lax.fori_loop(1, R * C, exchange, 0)
    own = [
        pltpu.make_async_copy(xv.at[2 * r, 2 * r], agr.at[row_spot], self_sem.at[0]),
        pltpu.make_async_copy(xv.at[2 * r + 1, 2 * r + 1], agr.at[row_spot + 1], self_sem.at[1]),
        pltpu.make_async_copy(xv.at[c, c], dcol.at[r * C + c], self_sem.at[2]),
        pltpu.make_async_copy(xv.at[pl.ds(2 * r, 2), c], land.at[pl.ds(2 * me, 2)], self_sem.at[3]),
    ]
    for copy in own:
        copy.start()

    for copy in own:
        copy.wait()
    piece = agr.at[pl.ds((p * 4 + q % 4) * 32, 32)]
    column_piece = dcol.at[pl.ds((r // 2) * 32, 32)]
    drain(agr.at[pl.ds(0, 30)], sr_recv)
    drain(dcol.at[pl.ds(0, 31)], sc_recv)

    def row_gather(k, carry):
        cc = (c // 8) * 8 + (c % 8 + 2 * k) % 8
        remote(piece, piece, ar_send, ar_recv, r, cc).start()
        return carry

    lax.fori_loop(1, 4, row_gather, 0)

    def col_gather(k, carry):
        remote(column_piece, column_piece, ac_send, ac_recv, (r + 2 * k) % R, c).start()
        return carry

    lax.fori_loop(1, 4, col_gather, 0)

    even = sub16 % 2 == 0
    worst = jnp.full((C, LANES), -1, I32)
    before = jnp.zeros((C, LANES), I32)
    for col in range(C):
        wanted = jnp.broadcast_to(ctb[r, col : col + 1, :], (C, LANES))
        seen = lookup(tt[col], mine % LANES)
        used = jnp.broadcast_to(count((seen == wanted) & (sub16 != col) & (sub16 != own_group)), (C, LANES))
        pair = jnp.where(even, used + pltpu.roll(used, C - 1, 0), 0)
        whole = jnp.sum(used, axis=0, keepdims=True)
        both = used + before if col % 2 else used
        before = used
        worst = jnp.maximum(worst, jnp.maximum(jnp.maximum(both - CAP_L, pair - CAP_R), whole - LANES))
    to_smem.wait()
    drain(land.at[pl.ds(0, 2 * (R * C - 1))], t1_recv)

    def pack_left(d, carry):
        for k in range(CAP_L):
            lpack[d * CAP_L + k] = land[jnp.clip(lists[8 + 2 * d, k], 0, 2 * R * C - 1)]
        return carry

    lax.fori_loop(0, R, pack_left, 0)
    def pack_right(d, carry):
        for k in range(CAP_R):
            rpack[d * CAP_R + k] = land[jnp.clip(lists[24 + d, k], 0, 2 * R * C - 1)]
        return carry

    lax.fori_loop(0, R, pack_right, 0)
    left_spot = pl.ds((p * R + q) * CAP_L, CAP_L)

    def send_left(chip):
        src = lpack.at[pl.ds(chip * CAP_L, CAP_L)]
        remote(src, lland.at[left_spot], xl_send, xl_recv, r, 2 * chip + p).start()

    right_spot = pl.ds(r * CAP_R, CAP_R)

    def send_right(rr):
        src = rpack.at[pl.ds(rr * CAP_R, CAP_R)]
        remote(src, rland.at[right_spot], xr_send, xr_recv, rr, c).start()

    source = q == r
    pl.when(jnp.logical_not(source))(functools.partial(send_left, r))
    pl.when(jnp.logical_not(source))(functools.partial(send_right, q))

    def send_left_rest(k, carry):
        chip = (q + k) % R
        pl.when(chip != r)(functools.partial(send_left, chip))
        return carry

    lax.fori_loop(1, R, send_left_rest, 0)
    keep_left = pltpu.make_async_copy(lpack.at[pl.ds(q * CAP_L, CAP_L)], lland.at[left_spot], self_sem.at[4])
    keep_left.start()

    def send_right_rest(k, carry):
        rr = (r + k) % R
        pl.when(rr != q)(functools.partial(send_right, rr))
        return carry

    lax.fori_loop(1, R, send_right_rest, 0)
    keep_right = pltpu.make_async_copy(rpack.at[right_spot], rland.at[right_spot], self_sem.at[5])
    keep_right.start()

    def collect(i, carry):
        panel[i] = land[jnp.clip(lists[0, i], 0, 2 * R * C - 1)]
        return carry

    lax.fori_loop(0, LANES, collect, 0, unroll=8)

    save = pltpu.make_async_copy(panel, panel_out, out_sem)
    save.start()

    drain(agr.at[pl.ds(0, 96)], ar_recv)
    forward = remote(agr.at[pl.ds(p * 128, 128)], agr.at[pl.ds(p * 128, 128)], fw_send, fw_recv, r, partner)
    forward.start()

    to_lanes(panel, tb)
    lane1 = iota((1, LANES), 1)
    group1 = 2 * r + lane1 // HALF

    def receive_pairs():
        keep_left.wait()
        drain(lland.at[pl.ds(0, (R - 1) * CAP_L)], xl_recv)
        left_half = lland.at[pl.ds(p * R * CAP_L, R * CAP_L)]
        share = remote(left_half, left_half, yl_send, yl_recv, r, partner)
        share.start()
        keep_right.wait()
        drain(rland.at[pl.ds(0, (R - 1) * CAP_R)], xr_recv)
        share.wait()

        def collect_pairs(i, carry):
            pair_a[i] = lland[jnp.clip(lists[3, i], 0, C * CAP_L - 1)]
            pair_b[i] = rland[jnp.clip(lists[4, i], 0, R * CAP_R - 1)]
            return carry

        lax.fori_loop(0, LANES, collect_pairs, 0, unroll=8)
        to_lanes(pair_a, pa)
        to_lanes(pair_b, pb)

    drain(dcol.at[pl.ds(0, 96)], ac_recv)

    def collect_column(i, carry):
        sorted_b[i] = dcol[jnp.clip(lists[2, i], 0, R * C - 1)]
        return carry

    lax.fori_loop(0, LANES, collect_column, 0, unroll=8)
    to_lanes(sorted_b, tc)
    block_products(tb, tc, ot, False)
    forward.wait()

    def collect_row(i, carry):
        sorted_a[i] = agr[jnp.clip(lists[1, i], 0, 2 * R * C - 1)]
        return carry

    lax.fori_loop(0, LANES, collect_row, 0, unroll=8)
    to_lanes(sorted_a, ta, (group1 != c).astype(F32))
    block_products(ta, tb, ot, True)

    @pl.when(source)
    def _():
        receive_pairs()
        own_terms, totals = jnp.zeros((BS, LANES), F32), jnp.zeros((BS, LANES), F32)
        for x in range(BS):
            own_terms = own_terms + tb[BS * x : BS * (x + 1), :] * tb[pl.ds(x, BS, stride=BS), :]
            totals = totals + pa[BS * x : BS * (x + 1), :] * pb[pl.ds(x, BS, stride=BS), :]
        diagonal = jnp.sum(own_terms, axis=0, keepdims=True)
        pairs = jnp.sum(totals, axis=0, keepdims=True)
        inside = jnp.broadcast_to((group1 == c).astype(BF16), (8, LANES))
        weight = lax.dot_general(inside, onehot[...], (((1,), (1,)), ((), ())), preferred_element_type=F32)
        partial = jnp.sum(
            jnp.where(group1 == c, diagonal, 0.0) + pairs * weight[0:1, :], axis=1, keepdims=True
        )
        most = jnp.max(jnp.max(worst, axis=0, keepdims=True), axis=1, keepdims=True).astype(F32)
        told = jnp.where(lane1 < HALF, jnp.broadcast_to(partial, (1, LANES)), jnp.broadcast_to(most, (1, LANES)))
        tr_row[p] = told

        def tell(k, carry):
            cc = (c + k) % C
            remote(tr_row.at[p], tr_row.at[p], tr_send, tr_recv, r, cc).start()
            return carry

        lax.fori_loop(1, C, tell, 0)

    pl.when(jnp.logical_not(source))(receive_pairs)

    block_products(pa, pb, tb, False)

    @pl.when(source)
    def _():
        drain(tr_row.at[pl.ds(0, 1)], tr_recv)
        drain(tr_all.at[pl.ds(0, C - 1)], tr_send)

    @pl.when(jnp.logical_not(source))
    def _():
        drain(tr_row, tr_recv)

    row_spot2 = pl.ds(2 * r, 2)

    def pass_on(k, carry):
        remote(tr_row, tr_all.at[row_spot2], tc_send, tc_recv, (r + k) % R, c).start()
        return carry

    lax.fori_loop(1, R, pass_on, 0)


    spread = onehot[...]
    for s in range(SUB):
        spot = slice(s * LANES, (s + 1) * LANES)
        value = tb[spot, :]
        high = value.astype(BF16)
        rest = value - high.astype(F32)
        middle = rest.astype(BF16)
        low = (rest - middle.astype(F32)).astype(BF16)
        moved = jnp.dot(low, spread, preferred_element_type=F32)
        moved = moved + jnp.dot(middle, spread, preferred_element_type=F32)
        moved = moved + jnp.dot(high, spread, preferred_element_type=F32)
        ot[spot, :] = ot[spot, :] + moved

    kept = keep[...].astype(F32)
    for s in range(SUB):
        spot = slice(s * LANES, (s + 1) * LANES)
        out[:, s, :] = jnp.transpose(ot[spot, :] * kept)

    drain(tr_all.at[pl.ds(0, 2 * (R - 1))], tc_recv)
    drain(tr_all.at[pl.ds(0, 2 * (R - 1))], tc_send)
    tr_all[row_spot2] = tr_row[...]
    trace, most = tr_all[0], tr_all[0]
    for k in range(1, C):
        trace = trace + tr_all[k]
        most = jnp.maximum(most, tr_all[k])
    mean_out[...] = trace[:, 0:1] / (R * LANES)
    over_out[...] = most[:, HALF : HALF + 1]

    save.wait()
    drain(agr.at[pl.ds(0, 30)], sr_send)
    drain(dcol.at[pl.ds(0, 31)], sc_send)
    drain(land.at[pl.ds(0, 2 * (R * C - 1))], t1_send)
    drain(agr.at[pl.ds(0, 96)], ar_send)
    drain(dcol.at[pl.ds(0, 96)], ac_send)
    drain(lland.at[pl.ds(0, (R - 1) * CAP_L)], xl_send)
    drain(rland.at[pl.ds(0, (R - 1) * CAP_R)], xr_send)


def sparse_product(blocks, cols, slots, keep):
    tile = (SUB, LANES)
    dma = pltpu.SemaphoreType.DMA
    wide = pltpu.VMEM((AREA, LANES), F32)
    batch = pltpu.VMEM((LANES,) + tile, F32)
    vmem = pl.BlockSpec(memory_space=pltpu.VMEM)
    hbm = pl.BlockSpec(memory_space=pl.ANY)
    return pl.pallas_call(
        kernel,
        out_shape=(
            jax.ShapeDtypeStruct((LANES,) + tile, F32),
            jax.ShapeDtypeStruct((1, 1), F32),
            jax.ShapeDtypeStruct((1, 1), F32),
            jax.ShapeDtypeStruct((LANES,) + tile, F32),
        ),
        in_specs=[hbm, hbm, vmem, vmem],
        out_specs=(vmem, vmem, vmem, hbm),
        scratch_shapes=[
            pltpu.VMEM((C, C) + tile, F32),
            pltpu.VMEM((2 * R * C,) + tile, F32),
            pltpu.VMEM((2 * R * C,) + tile, F32),
            pltpu.VMEM((R * C,) + tile, F32),
            pltpu.VMEM((R, C, LANES), I32),
            pltpu.VMEM((C, R, LANES), I32),
            pltpu.VMEM((C, C, LANES), I32),
            pltpu.VMEM((32, LANES), I32),
            pltpu.SMEM((32, LANES), I32),
            batch, batch, batch, batch, batch,
            wide, wide, wide, wide, wide, wide,
            pltpu.VMEM((R * CAP_L,) + tile, F32),
            pltpu.VMEM((R * CAP_R,) + tile, F32),
            pltpu.VMEM((C * CAP_L,) + tile, F32),
            pltpu.VMEM((R * CAP_R,) + tile, F32),
            pltpu.VMEM((LANES, LANES), BF16),
            pltpu.VMEM((2, 1, LANES), F32),
            pltpu.VMEM((C, 1, LANES), F32),
            dma((SUB,)), dma((4 * R,)), dma((6,)), dma, dma,
        ] + [dma] * 22,
        compiler_params=pltpu.CompilerParams(collective_id=0, has_side_effects=True),
    )(blocks, cols, slots, keep)


def dense_product(panel, columns, keep):
    r, c = lax.axis_index("row"), lax.axis_index("col")
    mine = lax.dynamic_slice_in_dim(columns, r * LANES, LANES)
    target = lax.dynamic_slice_in_dim(mine, c, 1, 1)[:, 0]
    far_all = lax.dynamic_slice_in_dim(columns, c, 1, 1)[:, 0]
    flat = panel.reshape(LANES, AREA)

    def around(value, axis):
        size = lax.axis_size(axis)
        return lax.ppermute(value, axis, [((i + 1) % size, i) for i in range(size)])

    def gather(step, carry):
        rights, moving = carry
        rights = lax.dynamic_update_slice_in_dim(rights, moving[None], (r + step) % R, 0)
        return rights, around(moving, "row")

    rights, _ = lax.fori_loop(0, R, gather, (jnp.zeros((R, LANES, AREA), F32), flat))
    rights = rights.reshape(R * LANES, AREA)

    def advance(step, carry):
        totals, left = carry
        m = (c + step) % C
        inner = lax.dynamic_slice_in_dim(mine, m, 1, 1)[:, 0]
        match = (far_all[inner] == target).astype(F32)
        right = rights[inner] * match[:, None]
        term = jnp.einsum(
            "nxz,nzy->nxy", left.reshape(LANES, BS, BS), right.reshape(LANES, BS, BS), precision=HIGHEST
        )
        return totals + term, around(left, "col")

    totals, _ = lax.fori_loop(0, C, advance, (jnp.zeros((LANES, BS, BS), F32), flat))
    ids = r * LANES + jnp.arange(LANES, dtype=I32)
    traces = jnp.trace(totals, axis1=1, axis2=2)
    trace = jnp.full((8, LANES), jnp.sum(jnp.where(target == ids, traces, 0.0)))
    for axis in ("row", "col"):
        def add(step, carry):
            total, moving = carry
            moving = around(moving, axis)
            return total + moving, moving
        trace, _ = lax.fori_loop(1, lax.axis_size(axis), add, (trace, trace))
    filtered = totals.reshape(LANES, AREA) * keep.reshape(LANES, 1).astype(F32)
    filtered = lax.optimization_barrier(filtered.reshape(SUB * LANES, LANES))
    return filtered, trace[0, 0] / (R * LANES)


def shards(blocks, columns, owner_slot, keep_mask):
    keep = keep_mask.T
    filtered, mean, over, panel = sparse_product(blocks, columns.T, owner_slot.reshape(R, LANES), keep)
    filtered, mean = lax.cond(
        over.reshape(()) > 0,
        lambda f, t, s: dense_product(s, columns, keep),
        lambda f, t, s: (f, t),
        filtered.reshape(SUB * LANES, LANES), mean.reshape(()), panel,
    )
    filtered = lax.optimization_barrier(filtered)
    return filtered.reshape(LANES, 1, AREA), mean


def solution(mesh):
    in_specs = (P(("row", "col"), None, None), P(), P(), P("row", "col"))
    out_specs = (P("row", "col", None), P())
    return jax.shard_map(shards, mesh=mesh, in_specs=in_specs, out_specs=out_specs, check_vma=False)
```

```python
import functools

import jax
import jax.numpy as jnp
from jax import lax
from jax.experimental import pallas as pl
from jax.experimental.pallas import tpu as pltpu
from jax.sharding import PartitionSpec as P

BS = 32
AREA = BS * BS
SUB, LANES = 8, 128
R, C = 8, 16
HALF = 64
CAP_L = 16
CAP_R = 16
CAP_T = 8
MESH = pl.DeviceIdType.MESH
F32, I32, BF16 = jnp.float32, jnp.int32, jnp.bfloat16
HIGHEST = lax.Precision.HIGHEST


def iota(shape, axis):
    return lax.broadcasted_iota(I32, shape, axis)


def lookup(table, index):
    return jnp.take_along_axis(table, index, axis=1, mode="promise_in_bounds")


def block_products(left, right, out, accumulate):
    def rows(step, carry):
        base = pl.multiple_of(step * (4 * BS), 4 * BS)
        totals = [[None] * 4 for _ in range(4)]
        for z in range(BS):
            tiles = [right[pl.ds(z * BS + 8 * q, 8), :] for q in range(4)]
            for x in range(4):
                factor = jnp.broadcast_to(left[pl.ds(base + x * BS + z, 1), :], (8, LANES))
                for q in range(4):
                    term = factor * tiles[q]
                    totals[x][q] = term if totals[x][q] is None else totals[x][q] + term
        for x in range(4):
            for q in range(4):
                spot = pl.ds(base + x * BS + 8 * q, 8)
                value = totals[x][q]
                out[spot, :] = out[spot, :] + value if accumulate else value
        return carry

    lax.fori_loop(0, BS // 4, rows, 0)


def to_lanes(stacked, out, keep=None):
    for s in range(SUB):
        piece = jnp.transpose(stacked[:, s, :])
        if keep is not None:
            piece = piece * keep
        out[s * LANES : (s + 1) * LANES, :] = piece


def kernel(
    blocks, cols, slots, keep,
    out, mean_out, over_out, panel_out,
    xv, land, agr, dcol, ctb, ct3, tt, lists_v, lists,
    panel, sorted_a, sorted_b, pair_a, pair_b, ta, tb, tc, pa, pb, ot,
    lpack, rpack, lland, rland, onehot, mpack, mland, tr_all,
    in_sem, ct_sem, self_sem, list_sem, out_sem,
    sr_send, sc_send, sr_recv, sc_recv,
    t1_send, t1_recv, ar_send, ac_send, ar_recv, ac_recv, fw_send, fw_recv,
    xl_send, xr_send, xl_recv, xr_recv, yl_send, yl_recv, tr_send, tr_recv, tc_send, tc_recv, m_send, m_recv,
):
    r = lax.axis_index("row")
    c = lax.axis_index("col")
    me = r * C + c
    p, q = c % 2, c // 2
    partner = c + 1 - 2 * p

    def remote(src, dst, send, recv, row, col):
        return pltpu.make_async_remote_copy(
            src_ref=src, dst_ref=dst, send_sem=send, recv_sem=recv,
            device_id=(row, col), device_id_type=MESH,
        )

    def drain(ref, sem):
        pltpu.make_async_copy(ref, ref, sem).wait()

    barrier = pltpu.get_barrier_semaphore()

    def greet(k, carry):
        d = (me + k) % (R * C)
        pl.semaphore_signal(barrier, inc=1, device_id=(d // C, d % C), device_id_type=MESH)
        return carry

    lax.fori_loop(1, R * C, greet, 0)

    loads = [
        pltpu.make_async_copy(blocks.at[:, :, pl.ds(LANES * t, LANES)], xv.at[:, :, t, :], in_sem.at[t])
        for t in range(SUB)
    ]
    for copy in loads:
        copy.start()
    tables = []
    for b in range(R):
        piece = cols.at[:, pl.ds(LANES * b, LANES)]
        tables.append(pltpu.make_async_copy(piece, ctb.at[b], ct_sem.at[4 * b]))
        tables.append(pltpu.make_async_copy(piece, ct3.at[:, b, :], ct_sem.at[4 * b + 1]))
        tables.append(pltpu.make_async_copy(piece, tt.at[:, 2 * b, :], ct_sem.at[4 * b + 2]))
        tables.append(pltpu.make_async_copy(piece, tt.at[:, 2 * b + 1, :], ct_sem.at[4 * b + 3]))
    for copy in tables:
        copy.start()

    for copy in tables:
        copy.wait()
    lane8, lane16 = iota((8, LANES), 1), iota((C, LANES), 1)
    sub8, sub16 = iota((8, LANES), 0), iota((C, LANES), 0)
    def prefix(value, axis):
        place, total, step = iota(value.shape, axis), value, 1
        while step < value.shape[axis]:
            total = total + jnp.where(place >= step, pltpu.roll(total, step, axis), 0)
            step *= 2
        return total - value

    def count_before(flags):
        return prefix(flags.astype(I32), 1)

    def count(flags):
        return jnp.sum(flags.astype(I32), axis=1, keepdims=True)

    own_group = 2 * r + (lane16 // HALF)
    mine = ctb[r]
    target = jnp.broadcast_to(ctb[r, pl.ds(c, 1), :], (C, LANES))
    found = lookup(tt[c], mine % LANES)
    hit = (found == target) & (sub16 != c) & (sub16 != own_group)
    rank = count_before(hit)
    total = jnp.broadcast_to(count(hit), (C, LANES))
    first = prefix(total, 0) + rank
    in_pair = jnp.where(sub16 % 2 == 1, pltpu.roll(total, 1, 0), 0) + rank
    ahead = c - p
    ahead_target = jnp.broadcast_to(ctb[r, pl.ds(ahead, 1), :], (C, LANES))
    ahead_hit = (lookup(tt[ahead], mine % LANES) == ahead_target) & (sub16 != ahead) & (sub16 != own_group)
    in_chip = rank + p * count(ahead_hit)
    spot_a = jnp.minimum(((sub16 % 2) * R + sub16 // 2) * CAP_L + in_chip, C * CAP_L - 1)
    spot_b = jnp.minimum((sub16 // 2) * CAP_R + in_pair, R * CAP_R - 1)
    spots = spot_a + 256 * spot_b
    rows = iota((LANES, LANES), 0)
    chosen = jnp.zeros((LANES, LANES), I32)
    picks = jnp.zeros((LANES, LANES), I32)
    order = jnp.where(hit, first, -1)
    for m in range(C):
        spread = rows == order[m : m + 1, :]
        chosen = jnp.where(spread, 1, chosen)
        picks = jnp.where(spread, spots[m : m + 1, :], picks)
    onehot[...] = chosen.astype(BF16)
    picks = jnp.broadcast_to(jnp.sum(picks, axis=1, keepdims=True), (LANES, LANES))
    picks = jnp.transpose(picks)[0:8, :]

    owner = slots[pl.ds(r, 1), :] // C
    far_owner = lookup(
        jnp.broadcast_to(slots[pl.ds(q, 1), :] // C, (8, LANES)),
        jnp.broadcast_to(ctb[r, pl.ds(c, 1), :] % LANES, (8, LANES)),
    )
    owner8 = jnp.broadcast_to(owner, (8, LANES))
    half = lane8 // HALF
    o_col, o_row = owner8 % C, owner8 // C
    at_land = 2 * owner8 + half
    at_agr = (((o_col % 2) * 4 + (o_col // 2) % 4) * 2 + o_col // 8) * 16 + o_row * 2 + half
    head = jnp.where(sub8 == 0, at_land, jnp.where(sub8 == 1, at_agr, far_owner))
    head = jnp.where(sub8 == 3, picks % 256, jnp.where(sub8 == 4, picks // 256, head))
    lists_v[0:8, :] = head

    left_index = jnp.broadcast_to(ctb[r, pl.ds(c, 1), :] % LANES, (C, LANES))
    left_found = lookup(ctb[q], left_index)
    left_hit = (left_found == mine) & (sub16 != c) & (own_group != c)
    left_rank = count_before(left_hit)
    left_total = jnp.broadcast_to(count(left_hit), (C, LANES))
    left_rank = left_rank + jnp.where(sub16 % 2 == 1, pltpu.roll(left_total, 1, 0), 0)
    at_land16 = jnp.broadcast_to(at_land[0:1, :], (C, LANES))
    left_list = jnp.zeros((C, LANES), I32)
    for k in range(CAP_L):
        value = jnp.sum(jnp.where(left_hit & (left_rank == k), at_land16, 0), axis=1, keepdims=True)
        left_list = jnp.where(lane16 == k, value, left_list)
    left_list = left_list + pltpu.roll(left_list, C - 1, 0)
    lists_v[8:24, :] = left_list

    right_target = ct3[c]
    right_table = jnp.broadcast_to(ct3[c, pl.ds(r, 1), :], (8, LANES))
    their_group = 2 * sub8 + half
    right_list = jnp.zeros((8, LANES), I32)
    flags, places, ranks = [], [], []
    for h in range(2):
        m = 2 * r + h
        place = ct3[m] % LANES
        right_hit = (lookup(right_table, place) == right_target) & (m != c) & (their_group != m)
        right_rank = count_before(right_hit)
        if h == 1:
            right_rank = right_rank + count(flags[0])
        flags.append(right_hit)
        places.append(lookup(at_land, place))
        ranks.append(right_rank)
    for k in range(CAP_R):
        value = sum(
            jnp.sum(jnp.where(flags[h] & (ranks[h] == k), places[h], 0), axis=1, keepdims=True)
            for h in range(2)
        )
        right_list = jnp.where(lane8 == k, value, right_list)
    lists_v[24:32, :] = right_list
    mutual_send, mutual_take, mutual_count = [], [], []
    for h in range(2):
        g = 2 * r + h
        own_place = jnp.broadcast_to(ct3[c, pl.ds(r, 1), :] % LANES, (8, LANES))
        back = lookup(jnp.broadcast_to(ct3[g, pl.ds(q, 1), :], (8, LANES)), own_place)
        ours = (back == LANES * r + lane8) & (half == h) & (c != g)
        ours_rank = count_before(ours)
        their_place = jnp.broadcast_to(ct3[g, pl.ds(q, 1), :] % LANES, (8, LANES))
        back = lookup(jnp.broadcast_to(ct3[c, pl.ds(r, 1), :], (8, LANES)), their_place)
        theirs = (back == LANES * q + lane8) & (half == p) & (c != g)
        theirs_rank = count_before(theirs)
        theirs_land = lookup(at_land, their_place)
        send_list, take_list = jnp.zeros((8, LANES), I32), jnp.zeros((8, LANES), I32)
        for k in range(CAP_T):
            value = jnp.sum(jnp.where(ours & (ours_rank == k), at_land, 0), axis=1, keepdims=True)
            send_list = jnp.where(lane8 == k, value, send_list)
            value = jnp.sum(jnp.where(theirs & (theirs_rank == k), theirs_land, 0), axis=1, keepdims=True)
            take_list = jnp.where(lane8 == k, value, take_list)
        mutual_send.append(send_list)
        mutual_take.append(take_list)
        mutual_count.append(jnp.broadcast_to(count(theirs), (8, LANES)))
    mutual = jnp.where(sub8 == 0, mutual_send[0], jnp.where(sub8 == 1, mutual_send[1], mutual_take[0]))
    lists_v[32:40, :] = jnp.where(sub8 == 3, mutual_take[1], mutual)
    to_smem = pltpu.make_async_copy(lists_v, lists, list_sem)
    to_smem.start()

    for copy in loads:
        copy.wait()
    pl.semaphore_wait(barrier, R * C - 1)

    row_spot = ((p * 4 + q % 4) * 2 + c // 8) * 16 + r * 2
    col_spot = r * C + c

    def row_scatter(k, carry):
        rr, cc = (r + k % R) % R, (c + 8 * (k // R)) % C
        for h in range(2):
            g = 2 * rr + h
            remote(xv.at[g, g], agr.at[row_spot + h], sr_send, sr_recv, rr, cc).start()
        return carry

    lax.fori_loop(1, 2 * R, row_scatter, 0)

    def col_scatter(k, carry):
        g, rr = (c + k % C) % C, r + (k // C) * (1 - 2 * (r % 2))
        remote(xv.at[g, g], dcol.at[col_spot], sc_send, sc_recv, rr, g).start()
        return carry

    lax.fori_loop(1, 2 * C, col_scatter, 0)

    def exchange(k, carry):
        d = (me + k * 37) % (R * C)
        rr, cc = d // C, d % C
        remote(xv.at[pl.ds(2 * rr, 2), cc], land.at[pl.ds(2 * me, 2)], t1_send, t1_recv, rr, cc).start()
        return carry

    lax.fori_loop(1, R * C, exchange, 0)
    own = [
        pltpu.make_async_copy(xv.at[2 * r, 2 * r], agr.at[row_spot], self_sem.at[0]),
        pltpu.make_async_copy(xv.at[2 * r + 1, 2 * r + 1], agr.at[row_spot + 1], self_sem.at[1]),
        pltpu.make_async_copy(xv.at[c, c], dcol.at[r * C + c], self_sem.at[2]),
        pltpu.make_async_copy(xv.at[pl.ds(2 * r, 2), c], land.at[pl.ds(2 * me, 2)], self_sem.at[3]),
    ]
    for copy in own:
        copy.start()

    for copy in own:
        copy.wait()
    piece = agr.at[pl.ds((p * 4 + q % 4) * 32, 32)]
    column_piece = dcol.at[pl.ds((r // 2) * 32, 32)]
    drain(agr.at[pl.ds(0, 30)], sr_recv)
    drain(dcol.at[pl.ds(0, 31)], sc_recv)

    def row_gather(k, carry):
        cc = (c // 8) * 8 + (c % 8 + 2 * k) % 8
        remote(piece, piece, ar_send, ar_recv, r, cc).start()
        return carry

    lax.fori_loop(1, 4, row_gather, 0)

    def col_gather(k, carry):
        remote(column_piece, column_piece, ac_send, ac_recv, (r + 2 * k) % R, c).start()
        return carry

    lax.fori_loop(1, 4, col_gather, 0)

    even = sub16 % 2 == 0
    worst = jnp.full((C, LANES), -1, I32)
    before = jnp.zeros((C, LANES), I32)
    for col in range(C):
        wanted = jnp.broadcast_to(ctb[r, col : col + 1, :], (C, LANES))
        seen = lookup(tt[col], mine % LANES)
        used = jnp.broadcast_to(count((seen == wanted) & (sub16 != col) & (sub16 != own_group)), (C, LANES))
        pair = jnp.where(even, used + pltpu.roll(used, C - 1, 0), 0)
        whole = jnp.sum(used, axis=0, keepdims=True)
        both = used + before if col % 2 else used
        before = used
        worst = jnp.maximum(worst, jnp.maximum(jnp.maximum(both - CAP_L, pair - CAP_R), whole - LANES))
    to_smem.wait()
    drain(land.at[pl.ds(0, 2 * (R * C - 1))], t1_recv)

    for h in range(2):
        for k in range(CAP_T):
            mpack[h * CAP_T + k] = land[jnp.clip(lists[32 + h, k], 0, 2 * R * C - 1)]
    diagonal_chip = q == r
    mine_spot = pl.ds(p * CAP_T, CAP_T)

    def send_mutual(h):
        remote(mpack.at[pl.ds(h * CAP_T, CAP_T)], mland.at[mine_spot], m_send, m_recv, q, 2 * r + h).start()

    for h in range(2):
        pl.when(jnp.logical_not(diagonal_chip & (p == h)))(functools.partial(send_mutual, h))

    def pack_left(d, carry):
        for k in range(CAP_L):
            lpack[d * CAP_L + k] = land[jnp.clip(lists[8 + 2 * d, k], 0, 2 * R * C - 1)]
        return carry

    lax.fori_loop(0, R, pack_left, 0)
    def pack_right(d, carry):
        for k in range(CAP_R):
            rpack[d * CAP_R + k] = land[jnp.clip(lists[24 + d, k], 0, 2 * R * C - 1)]
        return carry

    lax.fori_loop(0, R, pack_right, 0)
    left_spot = pl.ds((p * R + q) * CAP_L, CAP_L)

    def send_left(chip):
        src = lpack.at[pl.ds(chip * CAP_L, CAP_L)]
        remote(src, lland.at[left_spot], xl_send, xl_recv, r, 2 * chip + p).start()

    right_spot = pl.ds(r * CAP_R, CAP_R)

    def send_right(rr):
        src = rpack.at[pl.ds(rr * CAP_R, CAP_R)]
        remote(src, rland.at[right_spot], xr_send, xr_recv, rr, c).start()


    def send_left_rest(k, carry):
        send_left((q + k) % R)
        return carry

    lax.fori_loop(1, R, send_left_rest, 0)
    keep_left = pltpu.make_async_copy(lpack.at[pl.ds(q * CAP_L, CAP_L)], lland.at[left_spot], self_sem.at[4])
    keep_left.start()

    def send_right_rest(k, carry):
        send_right((r + k) % R)
        return carry

    lax.fori_loop(1, R, send_right_rest, 0)
    keep_right = pltpu.make_async_copy(rpack.at[right_spot], rland.at[right_spot], self_sem.at[5])
    keep_right.start()

    def collect(i, carry):
        panel[i] = land[jnp.clip(lists[0, i], 0, 2 * R * C - 1)]
        return carry

    lax.fori_loop(0, LANES, collect, 0, unroll=8)

    save = pltpu.make_async_copy(panel, panel_out, out_sem)
    save.start()

    drain(agr.at[pl.ds(0, 96)], ar_recv)
    forward = remote(agr.at[pl.ds(p * 128, 128)], agr.at[pl.ds(p * 128, 128)], fw_send, fw_recv, r, partner)
    forward.start()

    to_lanes(panel, tb)
    lane1 = iota((1, LANES), 1)
    group1 = 2 * r + lane1 // HALF

    def receive_pairs():
        keep_left.wait()
        drain(lland.at[pl.ds(0, (R - 1) * CAP_L)], xl_recv)
        left_half = lland.at[pl.ds(p * R * CAP_L, R * CAP_L)]
        share = remote(left_half, left_half, yl_send, yl_recv, r, partner)
        share.start()
        keep_right.wait()
        drain(rland.at[pl.ds(0, (R - 1) * CAP_R)], xr_recv)
        share.wait()

        def collect_pairs(i, carry):
            pair_a[i] = lland[jnp.clip(lists[3, i], 0, C * CAP_L - 1)]
            pair_b[i] = rland[jnp.clip(lists[4, i], 0, R * CAP_R - 1)]
            return carry

        lax.fori_loop(0, LANES, collect_pairs, 0, unroll=8)
        to_lanes(pair_a, pa)
        to_lanes(pair_b, pb)

    drain(dcol.at[pl.ds(0, 96)], ac_recv)

    def collect_column(i, carry):
        sorted_b[i] = dcol[jnp.clip(lists[2, i], 0, R * C - 1)]
        return carry

    lax.fori_loop(0, LANES, collect_column, 0, unroll=8)
    to_lanes(sorted_b, tc)
    block_products(tb, tc, ot, False)
    @pl.when(diagonal_chip)
    def _():
        drain(mland.at[pl.ds(0, CAP_T)], m_recv)

    @pl.when(jnp.logical_not(diagonal_chip))
    def _():
        drain(mland, m_recv)

    for t in range(2):
        for k in range(CAP_T):
            pair_a[t * CAP_T + k] = mland[t * CAP_T + k]
            pair_b[t * CAP_T + k] = land[jnp.clip(lists[34 + t, k], 0, 2 * R * C - 1)]
    to_lanes(pair_a, pa)
    to_lanes(pair_b, pb)
    own_terms, totals = jnp.zeros((BS, LANES), F32), jnp.zeros((BS, LANES), F32)
    for x in range(BS):
        own_terms = own_terms + tb[BS * x : BS * (x + 1), :] * tb[pl.ds(x, BS, stride=BS), :]
        totals = totals + pa[BS * x : BS * (x + 1), :] * pb[pl.ds(x, BS, stride=BS), :]
    squares = jnp.where(group1 == c, jnp.sum(own_terms, axis=0, keepdims=True), 0.0)
    filled = jnp.where(lane1 < CAP_T, mutual_count[0][0:1, :], mutual_count[1][0:1, :] + CAP_T)
    filled = (lane1 < filled) & (lane1 < 2 * CAP_T)
    pairs = jnp.where(filled, jnp.sum(totals, axis=0, keepdims=True), 0.0)
    partial = jnp.broadcast_to(jnp.sum(squares + pairs, axis=1, keepdims=True), (1, LANES))
    most = jnp.max(jnp.max(worst, axis=0, keepdims=True), axis=1, keepdims=True)
    most = jnp.maximum(jnp.broadcast_to(most, (1, LANES)), jnp.maximum(mutual_count[0], mutual_count[1])[0:1, :] - CAP_T)
    tr_all[me] = jnp.where(lane1 < HALF, partial, most.astype(F32))

    def tell(k, carry):
        remote(tr_all.at[me], tr_all.at[me], tr_send, tr_recv, r, (c + k) % C).start()
        return carry

    lax.fori_loop(1, C, tell, 0)

    forward.wait()

    def collect_row(i, carry):
        sorted_a[i] = agr[jnp.clip(lists[1, i], 0, 2 * R * C - 1)]
        return carry

    lax.fori_loop(0, LANES, collect_row, 0, unroll=8)
    to_lanes(sorted_a, ta, (group1 != c).astype(F32))
    block_products(ta, tb, ot, True)

    drain(tr_all.at[pl.ds(0, C - 1)], tr_recv)
    row_tiles = tr_all.at[pl.ds(C * r, C)]

    def pass_on(k, carry):
        remote(row_tiles, row_tiles, tc_send, tc_recv, (r + k) % R, c).start()
        return carry

    lax.fori_loop(1, R, pass_on, 0)

    receive_pairs()
    block_products(pa, pb, tb, False)

    spread = onehot[...]
    for s in range(SUB):
        spot = slice(s * LANES, (s + 1) * LANES)
        value = tb[spot, :]
        high = value.astype(BF16)
        rest = value - high.astype(F32)
        middle = rest.astype(BF16)
        low = (rest - middle.astype(F32)).astype(BF16)
        moved = jnp.dot(low, spread, preferred_element_type=F32)
        moved = moved + jnp.dot(middle, spread, preferred_element_type=F32)
        moved = moved + jnp.dot(high, spread, preferred_element_type=F32)
        ot[spot, :] = ot[spot, :] + moved

    kept = keep[...].astype(F32)
    for s in range(SUB):
        spot = slice(s * LANES, (s + 1) * LANES)
        out[:, s, :] = jnp.transpose(ot[spot, :] * kept)

    drain(tr_all.at[pl.ds(0, C * (R - 1))], tc_recv)
    tiles = tr_all[...]
    mean_out[...] = jnp.sum(tiles, axis=0)[:, 0:1] / (R * LANES)
    over_out[...] = jnp.max(tiles, axis=0)[:, HALF : HALF + 1]

    @pl.when(diagonal_chip)
    def _():
        drain(mland.at[pl.ds(0, CAP_T)], m_send)

    @pl.when(jnp.logical_not(diagonal_chip))
    def _():
        drain(mland, m_send)

    drain(tr_all.at[pl.ds(0, C - 1)], tr_send)
    drain(tr_all.at[pl.ds(0, C * (R - 1))], tc_send)
    save.wait()
    drain(agr.at[pl.ds(0, 30)], sr_send)
    drain(dcol.at[pl.ds(0, 31)], sc_send)
    drain(land.at[pl.ds(0, 2 * (R * C - 1))], t1_send)
    drain(agr.at[pl.ds(0, 96)], ar_send)
    drain(dcol.at[pl.ds(0, 96)], ac_send)
    drain(lland.at[pl.ds(0, (R - 1) * CAP_L)], xl_send)
    drain(rland.at[pl.ds(0, (R - 1) * CAP_R)], xr_send)


def sparse_product(blocks, cols, slots, keep):
    tile = (SUB, LANES)
    dma = pltpu.SemaphoreType.DMA
    wide = pltpu.VMEM((AREA, LANES), F32)
    batch = pltpu.VMEM((LANES,) + tile, F32)
    vmem = pl.BlockSpec(memory_space=pltpu.VMEM)
    hbm = pl.BlockSpec(memory_space=pl.ANY)
    return pl.pallas_call(
        kernel,
        out_shape=(
            jax.ShapeDtypeStruct((LANES,) + tile, F32),
            jax.ShapeDtypeStruct((1, 1), F32),
            jax.ShapeDtypeStruct((1, 1), F32),
            jax.ShapeDtypeStruct((LANES,) + tile, F32),
        ),
        in_specs=[hbm, hbm, vmem, vmem],
        out_specs=(vmem, vmem, vmem, hbm),
        scratch_shapes=[
            pltpu.VMEM((C, C) + tile, F32),
            pltpu.VMEM((2 * R * C,) + tile, F32),
            pltpu.VMEM((2 * R * C,) + tile, F32),
            pltpu.VMEM((R * C,) + tile, F32),
            pltpu.VMEM((R, C, LANES), I32),
            pltpu.VMEM((C, R, LANES), I32),
            pltpu.VMEM((C, C, LANES), I32),
            pltpu.VMEM((40, LANES), I32),
            pltpu.SMEM((40, LANES), I32),
            batch, batch, batch, batch, batch,
            wide, wide, wide, wide, wide, wide,
            pltpu.VMEM((R * CAP_L,) + tile, F32),
            pltpu.VMEM((R * CAP_R,) + tile, F32),
            pltpu.VMEM((C * CAP_L,) + tile, F32),
            pltpu.VMEM((R * CAP_R,) + tile, F32),
            pltpu.VMEM((LANES, LANES), BF16),
            pltpu.VMEM((2 * CAP_T,) + tile, F32),
            pltpu.VMEM((2 * CAP_T,) + tile, F32),
            pltpu.VMEM((R * C, 1, LANES), F32),
            dma((SUB,)), dma((4 * R,)), dma((6,)), dma, dma,
        ] + [dma] * 24,
        compiler_params=pltpu.CompilerParams(collective_id=0, has_side_effects=True),
    )(blocks, cols, slots, keep)


def dense_product(panel, columns, keep):
    r, c = lax.axis_index("row"), lax.axis_index("col")
    mine = lax.dynamic_slice_in_dim(columns, r * LANES, LANES)
    target = lax.dynamic_slice_in_dim(mine, c, 1, 1)[:, 0]
    far_all = lax.dynamic_slice_in_dim(columns, c, 1, 1)[:, 0]
    flat = panel.reshape(LANES, AREA)

    def around(value, axis):
        size = lax.axis_size(axis)
        return lax.ppermute(value, axis, [((i + 1) % size, i) for i in range(size)])

    def gather(step, carry):
        rights, moving = carry
        rights = lax.dynamic_update_slice_in_dim(rights, moving[None], (r + step) % R, 0)
        return rights, around(moving, "row")

    rights, _ = lax.fori_loop(0, R, gather, (jnp.zeros((R, LANES, AREA), F32), flat))
    rights = rights.reshape(R * LANES, AREA)

    def advance(step, carry):
        totals, left = carry
        m = (c + step) % C
        inner = lax.dynamic_slice_in_dim(mine, m, 1, 1)[:, 0]
        match = (far_all[inner] == target).astype(F32)
        right = rights[inner] * match[:, None]
        term = jnp.einsum(
            "nxz,nzy->nxy", left.reshape(LANES, BS, BS), right.reshape(LANES, BS, BS), precision=HIGHEST
        )
        return totals + term, around(left, "col")

    totals, _ = lax.fori_loop(0, C, advance, (jnp.zeros((LANES, BS, BS), F32), flat))
    ids = r * LANES + jnp.arange(LANES, dtype=I32)
    traces = jnp.trace(totals, axis1=1, axis2=2)
    trace = jnp.full((8, LANES), jnp.sum(jnp.where(target == ids, traces, 0.0)))
    for axis in ("row", "col"):
        def add(step, carry):
            total, moving = carry
            moving = around(moving, axis)
            return total + moving, moving
        trace, _ = lax.fori_loop(1, lax.axis_size(axis), add, (trace, trace))
    filtered = totals.reshape(LANES, AREA) * keep.reshape(LANES, 1).astype(F32)
    filtered = lax.optimization_barrier(filtered.reshape(SUB * LANES, LANES))
    return filtered, trace[0, 0] / (R * LANES)


def shards(blocks, columns, owner_slot, keep_mask):
    keep = keep_mask.T
    filtered, mean, over, panel = sparse_product(blocks, columns.T, owner_slot.reshape(R, LANES), keep)
    filtered, mean = lax.cond(
        over.reshape(()) > 0,
        lambda f, t, s: dense_product(s, columns, keep),
        lambda f, t, s: (f, t),
        filtered.reshape(SUB * LANES, LANES), mean.reshape(()), panel,
    )
    filtered = lax.optimization_barrier(filtered)
    return filtered.reshape(LANES, 1, AREA), mean


def solution(mesh):
    in_specs = (P(("row", "col"), None, None), P(), P(), P("row", "col"))
    out_specs = (P("row", "col", None), P())
    return jax.shard_map(shards, mesh=mesh, in_specs=in_specs, out_specs=out_specs, check_vma=False)
```

```python
import functools

import jax
import jax.numpy as jnp
from jax import lax
from jax.experimental import pallas as pl
from jax.experimental.pallas import tpu as pltpu
from jax.sharding import PartitionSpec as P

BS = 32
AREA = BS * BS
SUB, LANES = 8, 128
R, C = 8, 16
HALF = 64
CAP_L = 16
CAP_R = 16
MESH = pl.DeviceIdType.MESH
F32, I32, BF16 = jnp.float32, jnp.int32, jnp.bfloat16
HIGHEST = lax.Precision.HIGHEST


def iota(shape, axis):
    return lax.broadcasted_iota(I32, shape, axis)


def lookup(table, index):
    return jnp.take_along_axis(table, index, axis=1, mode="promise_in_bounds")


def block_products(left, right, out, accumulate):
    def rows(step, carry):
        base = pl.multiple_of(step * (4 * BS), 4 * BS)
        totals = [[None] * 4 for _ in range(4)]
        for z in range(BS):
            tiles = [right[pl.ds(z * BS + 8 * q, 8), :] for q in range(4)]
            for x in range(4):
                factor = jnp.broadcast_to(left[pl.ds(base + x * BS + z, 1), :], (8, LANES))
                for q in range(4):
                    term = factor * tiles[q]
                    totals[x][q] = term if totals[x][q] is None else totals[x][q] + term
        for x in range(4):
            for q in range(4):
                spot = pl.ds(base + x * BS + 8 * q, 8)
                value = totals[x][q]
                out[spot, :] = out[spot, :] + value if accumulate else value
        return carry

    lax.fori_loop(0, BS // 4, rows, 0)


def to_lanes(stacked, out, keep=None):
    for s in range(SUB):
        piece = jnp.transpose(stacked[:, s, :])
        if keep is not None:
            piece = piece * keep
        out[s * LANES : (s + 1) * LANES, :] = piece


def kernel(
    blocks, cols, slots, keep,
    out, mean_out, over_out, panel_out,
    xv, land, agr, dcol, ctb, ct3, tt, lists_v, lists,
    panel, sorted_a, sorted_b, pair_a, pair_b, ta, tb, tc, pa, pb, ot,
    lpack, rpack, lland, rland, onehot, tr_row, tr_all,
    in_sem, ct_sem, self_sem, list_sem, out_sem,
    sr_send, sc_send, sr_recv, sc_recv,
    t1_send, t1_recv, ar_send, ac_send, ar_recv, ac_recv, fw_send, fw_recv,
    xl_send, xr_send, xl_recv, xr_recv, yl_send, yl_recv, tr_send, tr_recv, tc_send, tc_recv,
):
    r = lax.axis_index("row")
    c = lax.axis_index("col")
    me = r * C + c
    p, q = c % 2, c // 2
    partner = c + 1 - 2 * p

    def remote(src, dst, send, recv, row, col):
        return pltpu.make_async_remote_copy(
            src_ref=src, dst_ref=dst, send_sem=send, recv_sem=recv,
            device_id=(row, col), device_id_type=MESH,
        )

    def drain(ref, sem):
        pltpu.make_async_copy(ref, ref, sem).wait()

    barrier = pltpu.get_barrier_semaphore()

    def greet(k, carry):
        d = (me + k) % (R * C)
        pl.semaphore_signal(barrier, inc=1, device_id=(d // C, d % C), device_id_type=MESH)
        return carry

    lax.fori_loop(1, R * C, greet, 0)

    loads = [
        pltpu.make_async_copy(blocks.at[:, :, pl.ds(LANES * t, LANES)], xv.at[:, :, t, :], in_sem.at[t])
        for t in range(SUB)
    ]
    for copy in loads:
        copy.start()
    tables = []
    for b in range(R):
        piece = cols.at[:, pl.ds(LANES * b, LANES)]
        tables.append(pltpu.make_async_copy(piece, ctb.at[b], ct_sem.at[4 * b]))
        tables.append(pltpu.make_async_copy(piece, ct3.at[:, b, :], ct_sem.at[4 * b + 1]))
        tables.append(pltpu.make_async_copy(piece, tt.at[:, 2 * b, :], ct_sem.at[4 * b + 2]))
        tables.append(pltpu.make_async_copy(piece, tt.at[:, 2 * b + 1, :], ct_sem.at[4 * b + 3]))
    for copy in tables:
        copy.start()

    for copy in tables:
        copy.wait()
    lane8, lane16 = iota((8, LANES), 1), iota((C, LANES), 1)
    sub8, sub16 = iota((8, LANES), 0), iota((C, LANES), 0)
    def prefix(value, axis):
        place, total, step = iota(value.shape, axis), value, 1
        while step < value.shape[axis]:
            total = total + jnp.where(place >= step, pltpu.roll(total, step, axis), 0)
            step *= 2
        return total - value

    def count_before(flags):
        return prefix(flags.astype(I32), 1)

    def count(flags):
        return jnp.sum(flags.astype(I32), axis=1, keepdims=True)

    own_group = 2 * r + (lane16 // HALF)
    mine = ctb[r]
    target = jnp.broadcast_to(ctb[r, pl.ds(c, 1), :], (C, LANES))
    found = lookup(tt[c], mine % LANES)
    hit = (found == target) & (sub16 != c) & (sub16 != own_group)
    rank = count_before(hit)
    total = jnp.broadcast_to(count(hit), (C, LANES))
    first = prefix(total, 0) + rank
    in_pair = jnp.where(sub16 % 2 == 1, pltpu.roll(total, 1, 0), 0) + rank
    ahead = c - p
    ahead_target = jnp.broadcast_to(ctb[r, pl.ds(ahead, 1), :], (C, LANES))
    ahead_hit = (lookup(tt[ahead], mine % LANES) == ahead_target) & (sub16 != ahead) & (sub16 != own_group)
    in_chip = rank + p * count(ahead_hit)
    spot_a = jnp.minimum(((sub16 % 2) * R + sub16 // 2) * CAP_L + in_chip, C * CAP_L - 1)
    spot_b = jnp.minimum((sub16 // 2) * CAP_R + in_pair, R * CAP_R - 1)
    spots = spot_a + 256 * spot_b
    rows = iota((LANES, LANES), 0)
    chosen = jnp.zeros((LANES, LANES), I32)
    picks = jnp.zeros((LANES, LANES), I32)
    order = jnp.where(hit, first, -1)
    for m in range(C):
        spread = rows == order[m : m + 1, :]
        chosen = jnp.where(spread, 1, chosen)
        picks = jnp.where(spread, spots[m : m + 1, :], picks)
    onehot[...] = chosen.astype(BF16)
    picks = jnp.broadcast_to(jnp.sum(picks, axis=1, keepdims=True), (LANES, LANES))
    picks = jnp.transpose(picks)[0:8, :]

    owner = slots[pl.ds(r, 1), :] // C
    far_owner = lookup(
        jnp.broadcast_to(slots[pl.ds(q, 1), :] // C, (8, LANES)),
        jnp.broadcast_to(ctb[r, pl.ds(c, 1), :] % LANES, (8, LANES)),
    )
    owner8 = jnp.broadcast_to(owner, (8, LANES))
    half = lane8 // HALF
    o_col, o_row = owner8 % C, owner8 // C
    at_land = 2 * owner8 + half
    at_agr = (((o_col % 2) * 4 + (o_col // 2) % 4) * 2 + o_col // 8) * 16 + o_row * 2 + half
    head = jnp.where(sub8 == 0, at_land, jnp.where(sub8 == 1, at_agr, far_owner))
    head = jnp.where(sub8 == 3, picks % 256, jnp.where(sub8 == 4, picks // 256, head))
    lists_v[0:8, :] = head

    left_index = jnp.broadcast_to(ctb[r, pl.ds(c, 1), :] % LANES, (C, LANES))
    left_found = lookup(ctb[q], left_index)
    left_hit = (left_found == mine) & (sub16 != c) & (own_group != c)
    left_rank = count_before(left_hit)
    left_total = jnp.broadcast_to(count(left_hit), (C, LANES))
    left_rank = left_rank + jnp.where(sub16 % 2 == 1, pltpu.roll(left_total, 1, 0), 0)
    at_land16 = jnp.broadcast_to(at_land[0:1, :], (C, LANES))
    left_list = jnp.zeros((C, LANES), I32)
    for k in range(CAP_L):
        value = jnp.sum(jnp.where(left_hit & (left_rank == k), at_land16, 0), axis=1, keepdims=True)
        left_list = jnp.where(lane16 == k, value, left_list)
    left_list = left_list + pltpu.roll(left_list, C - 1, 0)
    lists_v[8:24, :] = left_list

    right_target = ct3[c]
    right_table = jnp.broadcast_to(ct3[c, pl.ds(r, 1), :], (8, LANES))
    their_group = 2 * sub8 + half
    right_list = jnp.zeros((8, LANES), I32)
    flags, places, ranks = [], [], []
    for h in range(2):
        m = 2 * r + h
        place = ct3[m] % LANES
        right_hit = (lookup(right_table, place) == right_target) & (m != c) & (their_group != m)
        right_rank = count_before(right_hit)
        if h == 1:
            right_rank = right_rank + count(flags[0])
        flags.append(right_hit)
        places.append(lookup(at_land, place))
        ranks.append(right_rank)
    for k in range(CAP_R):
        value = sum(
            jnp.sum(jnp.where(flags[h] & (ranks[h] == k), places[h], 0), axis=1, keepdims=True)
            for h in range(2)
        )
        right_list = jnp.where(lane8 == k, value, right_list)
    lists_v[24:32, :] = right_list
    to_smem = pltpu.make_async_copy(lists_v, lists, list_sem)
    to_smem.start()

    for copy in loads:
        copy.wait()
    pl.semaphore_wait(barrier, R * C - 1)

    row_spot = ((p * 4 + q % 4) * 2 + c // 8) * 16 + r * 2
    col_spot = r * C + c

    def row_scatter(k, carry):
        rr, cc = (r + k % R) % R, (c + 8 * (k // R)) % C
        for h in range(2):
            g = 2 * rr + h
            remote(xv.at[g, g], agr.at[row_spot + h], sr_send, sr_recv, rr, cc).start()
        return carry

    lax.fori_loop(1, 2 * R, row_scatter, 0)

    def col_scatter(k, carry):
        g, rr = (c + k % C) % C, r + (k // C) * (1 - 2 * (r % 2))
        remote(xv.at[g, g], dcol.at[col_spot], sc_send, sc_recv, rr, g).start()
        return carry

    lax.fori_loop(1, 2 * C, col_scatter, 0)

    def exchange(k, carry):
        d = (me + k * 37) % (R * C)
        rr, cc = d // C, d % C
        remote(xv.at[pl.ds(2 * rr, 2), cc], land.at[pl.ds(2 * me, 2)], t1_send, t1_recv, rr, cc).start()
        return carry

    lax.fori_loop(1, 64, exchange, 0)
    own = [
        pltpu.make_async_copy(xv.at[2 * r, 2 * r], agr.at[row_spot], self_sem.at[0]),
        pltpu.make_async_copy(xv.at[2 * r + 1, 2 * r + 1], agr.at[row_spot + 1], self_sem.at[1]),
        pltpu.make_async_copy(xv.at[c, c], dcol.at[r * C + c], self_sem.at[2]),
        pltpu.make_async_copy(xv.at[pl.ds(2 * r, 2), c], land.at[pl.ds(2 * me, 2)], self_sem.at[3]),
    ]
    for copy in own:
        copy.start()

    for copy in own:
        copy.wait()
    piece = agr.at[pl.ds((p * 4 + q % 4) * 32, 32)]
    column_piece = dcol.at[pl.ds((r // 2) * 32, 32)]
    drain(agr.at[pl.ds(0, 30)], sr_recv)
    drain(dcol.at[pl.ds(0, 31)], sc_recv)

    def row_gather(k, carry):
        cc = (c // 8) * 8 + (c % 8 + 2 * k) % 8
        remote(piece, piece, ar_send, ar_recv, r, cc).start()
        return carry

    lax.fori_loop(1, 4, row_gather, 0)

    def col_gather(k, carry):
        remote(column_piece, column_piece, ac_send, ac_recv, (r + 2 * k) % R, c).start()
        return carry

    lax.fori_loop(1, 4, col_gather, 0)

    lax.fori_loop(64, R * C, exchange, 0)

    even = sub16 % 2 == 0
    worst = jnp.full((C, LANES), -1, I32)
    before = jnp.zeros((C, LANES), I32)
    for col in range(C):
        wanted = jnp.broadcast_to(ctb[r, col : col + 1, :], (C, LANES))
        seen = lookup(tt[col], mine % LANES)
        used = jnp.broadcast_to(count((seen == wanted) & (sub16 != col) & (sub16 != own_group)), (C, LANES))
        pair = jnp.where(even, used + pltpu.roll(used, C - 1, 0), 0)
        whole = jnp.sum(used, axis=0, keepdims=True)
        both = used + before if col % 2 else used
        before = used
        worst = jnp.maximum(worst, jnp.maximum(jnp.maximum(both - CAP_L, pair - CAP_R), whole - LANES))
    to_smem.wait()
    drain(land.at[pl.ds(0, 2 * (R * C - 1))], t1_recv)

    def pack_left(d, carry):
        for k in range(CAP_L):
            lpack[d * CAP_L + k] = land[jnp.clip(lists[8 + 2 * d, k], 0, 2 * R * C - 1)]
        return carry

    lax.fori_loop(0, R, pack_left, 0)
    def pack_right(d, carry):
        for k in range(CAP_R):
            rpack[d * CAP_R + k] = land[jnp.clip(lists[24 + d, k], 0, 2 * R * C - 1)]
        return carry

    lax.fori_loop(0, R, pack_right, 0)
    left_spot = pl.ds((p * R + q) * CAP_L, CAP_L)

    def send_left(chip):
        src = lpack.at[pl.ds(chip * CAP_L, CAP_L)]
        remote(src, lland.at[left_spot], xl_send, xl_recv, r, 2 * chip + p).start()

    right_spot = pl.ds(r * CAP_R, CAP_R)

    def send_right(rr):
        src = rpack.at[pl.ds(rr * CAP_R, CAP_R)]
        remote(src, rland.at[right_spot], xr_send, xr_recv, rr, c).start()

    source = q == r
    pl.when(jnp.logical_not(source))(functools.partial(send_left, r))
    pl.when(jnp.logical_not(source))(functools.partial(send_right, q))

    def send_left_rest(k, carry):
        chip = (q + k) % R
        pl.when(chip != r)(functools.partial(send_left, chip))
        return carry

    lax.fori_loop(1, R, send_left_rest, 0)
    keep_left = pltpu.make_async_copy(lpack.at[pl.ds(q * CAP_L, CAP_L)], lland.at[left_spot], self_sem.at[4])
    keep_left.start()

    def send_right_rest(k, carry):
        rr = (r + k) % R
        pl.when(rr != q)(functools.partial(send_right, rr))
        return carry

    lax.fori_loop(1, R, send_right_rest, 0)
    keep_right = pltpu.make_async_copy(rpack.at[right_spot], rland.at[right_spot], self_sem.at[5])
    keep_right.start()

    def collect(i, carry):
        panel[i] = land[jnp.clip(lists[0, i], 0, 2 * R * C - 1)]
        return carry

    lax.fori_loop(0, LANES, collect, 0, unroll=8)

    save = pltpu.make_async_copy(panel, panel_out, out_sem)
    save.start()

    drain(agr.at[pl.ds(0, 96)], ar_recv)
    forward = remote(agr.at[pl.ds(p * 128, 128)], agr.at[pl.ds(p * 128, 128)], fw_send, fw_recv, r, partner)
    forward.start()

    to_lanes(panel, tb)
    lane1 = iota((1, LANES), 1)
    group1 = 2 * r + lane1 // HALF

    def receive_pairs():
        keep_left.wait()
        drain(lland.at[pl.ds(0, (R - 1) * CAP_L)], xl_recv)
        left_half = lland.at[pl.ds(p * R * CAP_L, R * CAP_L)]
        share = remote(left_half, left_half, yl_send, yl_recv, r, partner)
        share.start()
        keep_right.wait()
        drain(rland.at[pl.ds(0, (R - 1) * CAP_R)], xr_recv)
        share.wait()

        def collect_pairs(i, carry):
            pair_a[i] = lland[jnp.clip(lists[3, i], 0, C * CAP_L - 1)]
            pair_b[i] = rland[jnp.clip(lists[4, i], 0, R * CAP_R - 1)]
            return carry

        lax.fori_loop(0, LANES, collect_pairs, 0, unroll=8)
        to_lanes(pair_a, pa)
        to_lanes(pair_b, pb)

    @pl.when(source)
    def _():
        receive_pairs()
        own_terms, totals = jnp.zeros((BS, LANES), F32), jnp.zeros((BS, LANES), F32)
        for x in range(BS):
            own_terms = own_terms + tb[BS * x : BS * (x + 1), :] * tb[pl.ds(x, BS, stride=BS), :]
            totals = totals + pa[BS * x : BS * (x + 1), :] * pb[pl.ds(x, BS, stride=BS), :]
        diagonal = jnp.sum(own_terms, axis=0, keepdims=True)
        pairs = jnp.sum(totals, axis=0, keepdims=True)
        inside = jnp.broadcast_to((group1 == c).astype(BF16), (8, LANES))
        weight = lax.dot_general(inside, onehot[...], (((1,), (1,)), ((), ())), preferred_element_type=F32)
        partial = jnp.sum(
            jnp.where(group1 == c, diagonal, 0.0) + pairs * weight[0:1, :], axis=1, keepdims=True
        )
        most = jnp.max(jnp.max(worst, axis=0, keepdims=True), axis=1, keepdims=True).astype(F32)
        told = jnp.where(lane1 < HALF, jnp.broadcast_to(partial, (1, LANES)), jnp.broadcast_to(most, (1, LANES)))
        tr_row[p] = told

        def tell(k, carry):
            cc = (c + k) % C
            remote(tr_row.at[p], tr_row.at[p], tr_send, tr_recv, r, cc).start()
            return carry

        lax.fori_loop(1, C, tell, 0)

    drain(dcol.at[pl.ds(0, 96)], ac_recv)

    def collect_column(i, carry):
        sorted_b[i] = dcol[jnp.clip(lists[2, i], 0, R * C - 1)]
        return carry

    lax.fori_loop(0, LANES, collect_column, 0, unroll=8)
    to_lanes(sorted_b, tc)
    block_products(tb, tc, ot, False)
    forward.wait()

    def collect_row(i, carry):
        sorted_a[i] = agr[jnp.clip(lists[1, i], 0, 2 * R * C - 1)]
        return carry

    lax.fori_loop(0, LANES, collect_row, 0, unroll=8)
    to_lanes(sorted_a, ta, (group1 != c).astype(F32))
    block_products(ta, tb, ot, True)

    @pl.when(source)
    def _():
        drain(tr_row.at[pl.ds(0, 1)], tr_recv)
        drain(tr_all.at[pl.ds(0, C - 1)], tr_send)

    @pl.when(jnp.logical_not(source))
    def _():
        drain(tr_row, tr_recv)

    row_spot2 = pl.ds(2 * r, 2)

    def pass_on(k, carry):
        remote(tr_row, tr_all.at[row_spot2], tc_send, tc_recv, (r + k) % R, c).start()
        return carry

    lax.fori_loop(1, R, pass_on, 0)

    pl.when(jnp.logical_not(source))(receive_pairs)

    block_products(pa, pb, tb, False)

    spread = onehot[...]
    for s in range(SUB):
        spot = slice(s * LANES, (s + 1) * LANES)
        value = tb[spot, :]
        high = value.astype(BF16)
        rest = value - high.astype(F32)
        middle = rest.astype(BF16)
        low = (rest - middle.astype(F32)).astype(BF16)
        moved = jnp.dot(low, spread, preferred_element_type=F32)
        moved = moved + jnp.dot(middle, spread, preferred_element_type=F32)
        moved = moved + jnp.dot(high, spread, preferred_element_type=F32)
        ot[spot, :] = ot[spot, :] + moved

    kept = keep[...].astype(F32)
    for s in range(SUB):
        spot = slice(s * LANES, (s + 1) * LANES)
        out[:, s, :] = jnp.transpose(ot[spot, :] * kept)

    drain(tr_all.at[pl.ds(0, 2 * (R - 1))], tc_recv)
    drain(tr_all.at[pl.ds(0, 2 * (R - 1))], tc_send)
    tr_all[row_spot2] = tr_row[...]
    trace, most = tr_all[0], tr_all[0]
    for k in range(1, C):
        trace = trace + tr_all[k]
        most = jnp.maximum(most, tr_all[k])
    mean_out[...] = trace[:, 0:1] / (R * LANES)
    over_out[...] = most[:, HALF : HALF + 1]

    save.wait()
    drain(agr.at[pl.ds(0, 30)], sr_send)
    drain(dcol.at[pl.ds(0, 31)], sc_send)
    drain(land.at[pl.ds(0, 2 * (R * C - 1))], t1_send)
    drain(agr.at[pl.ds(0, 96)], ar_send)
    drain(dcol.at[pl.ds(0, 96)], ac_send)
    drain(lland.at[pl.ds(0, (R - 1) * CAP_L)], xl_send)
    drain(rland.at[pl.ds(0, (R - 1) * CAP_R)], xr_send)


def sparse_product(blocks, cols, slots, keep):
    tile = (SUB, LANES)
    dma = pltpu.SemaphoreType.DMA
    wide = pltpu.VMEM((AREA, LANES), F32)
    batch = pltpu.VMEM((LANES,) + tile, F32)
    vmem = pl.BlockSpec(memory_space=pltpu.VMEM)
    hbm = pl.BlockSpec(memory_space=pl.ANY)
    return pl.pallas_call(
        kernel,
        out_shape=(
            jax.ShapeDtypeStruct((LANES,) + tile, F32),
            jax.ShapeDtypeStruct((1, 1), F32),
            jax.ShapeDtypeStruct((1, 1), F32),
            jax.ShapeDtypeStruct((LANES,) + tile, F32),
        ),
        in_specs=[hbm, hbm, vmem, vmem],
        out_specs=(vmem, vmem, vmem, hbm),
        scratch_shapes=[
            pltpu.VMEM((C, C) + tile, F32),
            pltpu.VMEM((2 * R * C,) + tile, F32),
            pltpu.VMEM((2 * R * C,) + tile, F32),
            pltpu.VMEM((R * C,) + tile, F32),
            pltpu.VMEM((R, C, LANES), I32),
            pltpu.VMEM((C, R, LANES), I32),
            pltpu.VMEM((C, C, LANES), I32),
            pltpu.VMEM((32, LANES), I32),
            pltpu.SMEM((32, LANES), I32),
            batch, batch, batch, batch, batch,
            wide, wide, wide, wide, wide, wide,
            pltpu.VMEM((R * CAP_L,) + tile, F32),
            pltpu.VMEM((R * CAP_R,) + tile, F32),
            pltpu.VMEM((C * CAP_L,) + tile, F32),
            pltpu.VMEM((R * CAP_R,) + tile, F32),
            pltpu.VMEM((LANES, LANES), BF16),
            pltpu.VMEM((2, 1, LANES), F32),
            pltpu.VMEM((C, 1, LANES), F32),
            dma((SUB,)), dma((4 * R,)), dma((6,)), dma, dma,
        ] + [dma] * 22,
        compiler_params=pltpu.CompilerParams(collective_id=0, has_side_effects=True),
    )(blocks, cols, slots, keep)


def dense_product(panel, columns, keep):
    r, c = lax.axis_index("row"), lax.axis_index("col")
    mine = lax.dynamic_slice_in_dim(columns, r * LANES, LANES)
    target = lax.dynamic_slice_in_dim(mine, c, 1, 1)[:, 0]
    far_all = lax.dynamic_slice_in_dim(columns, c, 1, 1)[:, 0]
    flat = panel.reshape(LANES, AREA)

    def around(value, axis):
        size = lax.axis_size(axis)
        return lax.ppermute(value, axis, [((i + 1) % size, i) for i in range(size)])

    def gather(step, carry):
        rights, moving = carry
        rights = lax.dynamic_update_slice_in_dim(rights, moving[None], (r + step) % R, 0)
        return rights, around(moving, "row")

    rights, _ = lax.fori_loop(0, R, gather, (jnp.zeros((R, LANES, AREA), F32), flat))
    rights = rights.reshape(R * LANES, AREA)

    def advance(step, carry):
        totals, left = carry
        m = (c + step) % C
        inner = lax.dynamic_slice_in_dim(mine, m, 1, 1)[:, 0]
        match = (far_all[inner] == target).astype(F32)
        right = rights[inner] * match[:, None]
        term = jnp.einsum(
            "nxz,nzy->nxy", left.reshape(LANES, BS, BS), right.reshape(LANES, BS, BS), precision=HIGHEST
        )
        return totals + term, around(left, "col")

    totals, _ = lax.fori_loop(0, C, advance, (jnp.zeros((LANES, BS, BS), F32), flat))
    ids = r * LANES + jnp.arange(LANES, dtype=I32)
    traces = jnp.trace(totals, axis1=1, axis2=2)
    trace = jnp.full((8, LANES), jnp.sum(jnp.where(target == ids, traces, 0.0)))
    for axis in ("row", "col"):
        def add(step, carry):
            total, moving = carry
            moving = around(moving, axis)
            return total + moving, moving
        trace, _ = lax.fori_loop(1, lax.axis_size(axis), add, (trace, trace))
    filtered = totals.reshape(LANES, AREA) * keep.reshape(LANES, 1).astype(F32)
    filtered = lax.optimization_barrier(filtered.reshape(SUB * LANES, LANES))
    return filtered, trace[0, 0] / (R * LANES)


def shards(blocks, columns, owner_slot, keep_mask):
    keep = keep_mask.T
    filtered, mean, over, panel = sparse_product(blocks, columns.T, owner_slot.reshape(R, LANES), keep)
    filtered, mean = lax.cond(
        over.reshape(()) > 0,
        lambda f, t, s: dense_product(s, columns, keep),
        lambda f, t, s: (f, t),
        filtered.reshape(SUB * LANES, LANES), mean.reshape(()), panel,
    )
    filtered = lax.optimization_barrier(filtered)
    return filtered.reshape(LANES, 1, AREA), mean


def solution(mesh):
    in_specs = (P(("row", "col"), None, None), P(), P(), P("row", "col"))
    out_specs = (P("row", "col", None), P())
    return jax.shard_map(shards, mesh=mesh, in_specs=in_specs, out_specs=out_specs, check_vma=False)
```
